128 devices in a mesh: lon: 32 (over y, z, x_lo), ch: 4 (over x_hi, core).
Axes of the slice: x: 4 (x_hi: 2, x_lo: 2; x = x_hi * 2 + x_lo), y: 4, z: 4, core: 2. Of those that a mesh axis runs over, the one named last changes fastest.
Arguments:
- features: bfloat16 [1024, 1, 576, 128], P('ch', None, 'lon'), may hold values from -6 to 6
- cotangent: bfloat16 [3, 256, 1, 576, 128], P(None, 'ch', None, 'lon'), may hold values from -6 to 6
- weights: bfloat16 [3, 3, 3, 256, 1024], P(None, None, None, 'ch'), may hold values from -0.0625 to 0.0625
Outputs:
- input_grad: bfloat16 [1024, 1, 576, 128], P('ch', None, 'lon')
- kernel_grad: float32 [3, 3, 3, 256, 1024], P(None, None, None, 'ch')
The draws below stay inside these ranges and needn't reach their ends.
All inputs are finite; a program needn't handle non-finite values.
Results may differ from the reference program's by a relative error of at most 0.001.
Values may be sent and summed in bfloat16 or wider, within the bound.
A program may use at most 256 MiB of HBM per device.

```python
import jax
import jax.numpy as jnp

IN_CH = 1024
OUT_CH = 256
BATCH = 1
ROWS = 128
LON = 576


def block_levels(own_key, dims, shards, least, largest):
    def one(axis_at, shards_of):
        draws = jax.random.uniform(jax.random.fold_in(jax.random.fold_in(own_key, 6), axis_at), (shards_of,), jnp.float32, least / len(shards), largest / len(shards))
        return jnp.repeat(jnp.exp(draws), dims[axis_at] // shards_of).reshape((-1,) + (1,) * (len(dims) - axis_at - 1))

    level = one(*shards[0])
    for cut in shards[1:]:
        level = level * one(*cut)
    return level


def normal_values(own_key, extent, width, bound, cuts=(), held_as=jnp.bfloat16):
    values = width * jax.random.normal(own_key, extent, jnp.float32)
    if cuts:
        values = values * block_levels(own_key, extent, cuts, -0.22, 0.18)
    return jnp.clip(values, -bound, bound).astype(held_as)


def setup_inputs(seed: int = 0) -> dict:
    key_of = jax.random.split(jax.random.key(seed), 4)
    return {
        "features": normal_values(key_of[0], (IN_CH, BATCH, LON, ROWS), 1.0, 6.0, ((0, 4), (2, 32))),
        "cotangent": normal_values(key_of[1], (3, OUT_CH, BATCH, LON, ROWS), 1.0, 6.0, ((1, 4), (3, 32))),
        "weights": normal_values(key_of[2], (3, 3, 3, OUT_CH, IN_CH), (9 * IN_CH) ** -0.5, 0.0625, ((3, 4),)),
    }


DILATIONS = (6, 12, 18)

def reference(features, cotangent, weights):
    feat = features.astype(jnp.float32)
    grads = cotangent.astype(jnp.float32)
    kernels = weights.astype(jnp.float32)
    cells = BATCH * LON * ROWS
    input_sum = jnp.zeros((IN_CH, cells), jnp.float32)
    kernel_list = []
    for branch in range(3):
        dilation = DILATIONS[branch]
        grad_here = grads[branch]
        grad_pad = jnp.pad(grad_here, ((0, 0), (0, 0), (0, 0), (dilation, dilation)))
        feat_pad = jnp.pad(feat, ((0, 0), (0, 0), (0, 0), (dilation, dilation)))
        flat_grad = grad_here.reshape(OUT_CH, cells)
        for lat_tap in range(3):
            for lon_tap in range(3):
                lat_off = dilation * (lat_tap - 1)
                lon_off = dilation * (lon_tap - 1)
                shifted = jnp.roll(feat_pad, -lon_off, axis=2)[:, :, :, dilation + lat_off:dilation + lat_off + ROWS]
                kernel_list.append(jnp.dot(flat_grad, shifted.reshape(IN_CH, cells).T, preferred_element_type=jnp.float32))
                moved = jnp.roll(grad_pad, lon_off, axis=2)[:, :, :, dilation - lat_off:dilation - lat_off + ROWS]
                input_sum = input_sum + jnp.dot(kernels[branch, lat_tap, lon_tap].T, moved.reshape(OUT_CH, cells), preferred_element_type=jnp.float32)
    kernel_grad = jnp.stack(kernel_list).reshape(3, 3, 3, OUT_CH, IN_CH) / jnp.sqrt(jnp.float32(cells))
    input_grad = input_sum.reshape(IN_CH, BATCH, LON, ROWS).astype(jnp.bfloat16)
    return (input_grad, kernel_grad)
```

```python
import jax
import jax.numpy as jnp
from jax import lax
from jax.experimental import pallas as pl
from jax.experimental.pallas import tpu as pltpu
from jax.sharding import PartitionSpec as P

DILATIONS = (6, 12, 18)


def widened_branches(cotangent):
    count = lax.axis_size("lon")
    cols = cotangent.shape[3]
    tails = jnp.concatenate([cotangent[k, :, 0, cols - d :] for k, d in enumerate(DILATIONS)], axis=1)
    heads = jnp.concatenate([cotangent[k, :, 0, :d] for k, d in enumerate(DILATIONS)], axis=1)
    before = lax.ppermute(tails, "lon", [(i, (i + 1) % count) for i in range(count)])
    after = lax.ppermute(heads, "lon", [((i + 1) % count, i) for i in range(count)])
    wide = []
    start = 0
    for k, d in enumerate(DILATIONS):
        wide.append(
            jnp.concatenate([before[:, start : start + d], cotangent[k, :, 0], after[:, start : start + d]], axis=1)
        )
        start += d
    return wide


def tap_stack(wide, lon_cols, lat_rows):
    slices = []
    for k, d in enumerate(DILATIONS):
        padded = jnp.pad(wide[k], ((0, 0), (0, 0), (d, d)))
        for lat_tap in range(3):
            for lon_tap in range(3):
                lon_start = d - d * (lon_tap - 1)
                lat_start = d - d * (lat_tap - 1)
                slices.append(padded[:, lon_start : lon_start + lon_cols, lat_start : lat_start + lat_rows])
    return jnp.concatenate(slices, axis=0)


MESH = pl.DeviceIdType.MESH
Y, Z, X = 4, 4, 2


def sum_kernel(part, out, acc, first, second, third, low, load_sem, send_sem, recv_sem):
    lon = lax.axis_index("lon")
    ch = lax.axis_index("ch")
    y, z, x = lon // (Z * X), (lon // X) % Z, lon % X
    rows, half = acc.shape[1], acc.shape[2]
    strip = half // 4
    low_rows = rows // 2

    def at(dy, dz, dx):
        place = lax.rem(y + dy, Y) * (Z * X) + lax.rem(z + dz, Z) * X + lax.rem(x + dx, X)
        return (place, ch)

    hops = [(d, 0, 0) for d in (1, 2, 3)], [(0, d, 0) for d in (1, 2, 3)]
    barrier = pltpu.get_barrier_semaphore()
    for hop in hops[0] + hops[1] + [(0, 0, 1)]:
        pl.semaphore_signal(barrier, inc=1, device_id=at(*hop), device_id_type=MESH)
    pl.semaphore_wait(barrier, 7)

    here = (y, z)

    def block(h, row_block):
        return pl.ds(pl.multiple_of(row_block * rows, 8), rows), pl.ds(h * half, half)

    def push(src, dst, slot, hop):
        copy = pltpu.make_async_remote_copy(
            src_ref=src,
            dst_ref=dst,
            send_sem=send_sem.at[slot],
            recv_sem=recv_sem.at[slot],
            device_id=at(*hop),
            device_id_type=MESH,
        )
        copy.start()
        return copy

    stage = [[], []]
    for d in range(3):
        for h in range(2):
            there = block(h, lax.rem(here[h] + d + 1, 4))
            stage[h].append(push(part.at[there], first.at[h, d], h * 3 + d, hops[h][d]))
    loads = []
    for h in range(2):
        load = pltpu.make_async_copy(part.at[block(h, here[h])], acc.at[h], load_sem.at[h])
        load.start()
        loads.append(load)

    def add_first(h):
        def step(i, carry):
            at_rows = pl.ds(pl.multiple_of(i * 16, 16), 16)
            acc[h, at_rows, :] = (acc[h, at_rows, :] + first[h, 0, at_rows, :]) + (
                first[h, 1, at_rows, :] + first[h, 2, at_rows, :]
            )
            return carry

        lax.fori_loop(0, rows // 16, step, 0)

    stage2 = [[], []]
    for h in range(2):
        loads[h].wait()
        for copy in stage[h]:
            copy.wait()
        add_first(h)
        other = here[1 - h]
        for d in range(3):
            cols = pl.ds(pl.multiple_of(lax.rem(other + d + 1, 4) * strip, strip), strip)
            stage2[h].append(push(acc.at[h, :, cols], second.at[h, d], 6 + h * 3 + d, hops[1 - h][d]))

    stage3 = []
    for h in range(2):
        for copy in stage2[h]:
            copy.wait()
        cols = pl.ds(pl.multiple_of(here[1 - h] * strip, strip), strip)

        def step(i, carry):
            at_rows = pl.ds(pl.multiple_of(i * 16, 16), 16)
            second[h, 0, at_rows, :] = (acc[h, at_rows, cols] + second[h, 0, at_rows, :]) + (
                second[h, 1, at_rows, :] + second[h, 2, at_rows, :]
            )
            return carry

        lax.fori_loop(0, rows // 16, step, 0)
        theirs = pl.ds(pl.multiple_of((1 - x) * low_rows, 8), low_rows)
        stage3.append(push(second.at[h, 0, theirs], third.at[h], 12 + h, (0, 0, 1)))

    def corner(h):
        start = here[h] * rows + x * low_rows
        return (
            pl.ds(pl.multiple_of(start, 8), low_rows),
            pl.ds(pl.multiple_of(h * half + here[1 - h] * strip, strip), strip),
        )

    stores, back = [], []
    for h in range(2):
        stage3[h].wait()

        def step(i, carry):
            at_rows = pl.ds(pl.multiple_of(i * 8, 8), 8)
            mine = pl.ds(pl.multiple_of(x * low_rows + i * 8, 8), 8)
            low[h, at_rows, :] = second[h, 0, mine, :] + third[h, at_rows, :]
            return carry

        lax.fori_loop(0, low_rows // 8, step, 0)
        store = pltpu.make_async_copy(low.at[h], out.at[corner(h)], load_sem.at[2 + h])
        store.start()
        stores.append(store)
        back.append(push(low.at[h], out.at[corner(h)], 14 + h, (0, 0, 1)))

    back2 = [[], []]
    for h in range(2):
        stores[h].wait()
        back[h].wait()
        area = (
            pl.ds(pl.multiple_of(here[h] * rows, 8), rows),
            pl.ds(pl.multiple_of(h * half + here[1 - h] * strip, strip), strip),
        )
        for d in range(3):
            back2[h].append(push(out.at[area], out.at[area], 16 + h * 3 + d, hops[1 - h][d]))
    back3 = [[], []]
    for h in range(2):
        for copy in back2[h]:
            copy.wait()
        area = block(h, here[h])
        for d in range(3):
            back3[h].append(push(out.at[area], out.at[area], 22 + h * 3 + d, hops[h][d]))
    for h in range(2):
        for copy in back3[h]:
            copy.wait()


def sum_over_lon(part):
    total, cols = part.shape
    rows, half = total // 4, cols // 2
    return pl.pallas_call(
        sum_kernel,
        out_shape=jax.ShapeDtypeStruct(part.shape, part.dtype),
        in_specs=[pl.BlockSpec(memory_space=pl.ANY)],
        out_specs=pl.BlockSpec(memory_space=pl.ANY),
        scratch_shapes=[
            pltpu.VMEM((2, rows, half), jnp.float32),
            pltpu.VMEM((2, 3, rows, half), jnp.float32),
            pltpu.VMEM((2, 3, rows, half // 4), jnp.float32),
            pltpu.VMEM((2, rows // 2, half // 4), jnp.float32),
            pltpu.VMEM((2, rows // 2, half // 4), jnp.float32),
            pltpu.SemaphoreType.DMA((4,)),
            pltpu.SemaphoreType.DMA((28,)),
            pltpu.SemaphoreType.DMA((28,)),
        ],
        compiler_params=pltpu.CompilerParams(
            collective_id=1, has_side_effects=True, vmem_limit_bytes=24 * 1024 * 1024
        ),
        cost_estimate=pl.CostEstimate(flops=8 * total * cols, bytes_accessed=40 * total * cols * 4, transcendentals=0),
        name="sum_over_lon",
    )(part)


def local(features, cotangent, weights):
    in_rows = features.shape[0]
    in_total = weights.shape[4]
    out_rows = weights.shape[3]
    lon_cols = features.shape[2]
    lat_rows = features.shape[3]
    cells = lon_cols * lat_rows
    whole = lax.all_gather(features, "ch", axis=0, tiled=True).reshape(in_total, cells)
    stack = tap_stack(widened_branches(cotangent), lon_cols, lat_rows).reshape(-1, cells)
    partial_kernel = lax.dot_general(stack, whole, (((1,), (1,)), ((), ())), preferred_element_type=jnp.float32)
    product = lax.dot_general(
        weights.reshape(-1, in_total), stack, (((0,), (0,)), ((), ())), preferred_element_type=jnp.float32
    )
    partial_kernel, product = lax.optimization_barrier((partial_kernel, product))
    input_grad = (
        lax.psum_scatter(product, "ch", scatter_dimension=0, tiled=True)
        .astype(jnp.bfloat16)
        .reshape(in_rows, 1, lon_cols, lat_rows)
    )
    kernel_grad = sum_over_lon(partial_kernel) / jnp.sqrt(jnp.float32(cells * lax.axis_size("lon")))
    kernel_grad = kernel_grad.reshape(3, 3, 3, out_rows, in_total)
    return (input_grad, kernel_grad)


def solution(mesh):
    return jax.shard_map(
        local,
        mesh=mesh,
        in_specs=(
            P("ch", None, "lon", None),
            P(None, "ch", None, "lon", None),
            P(None, None, None, "ch", None),
        ),
        out_specs=(P("ch", None, "lon", None), P(None, None, None, "ch", None)),
        check_vma=False,
    )
```

```python
import functools
import math

import jax
import jax.numpy as jnp
from jax import lax
from jax.experimental import pallas as pl
from jax.experimental.pallas import tpu as pltpu
from jax.sharding import PartitionSpec as P

DILATIONS = (6, 12, 18)
BASES = (0, 30, 72)
MESH = pl.DeviceIdType.MESH
Y, Z, X = 4, 4, 2
CHUNKS = 6


def mod4(v):
    return lax.rem(v, 4)


def aligned(v, m, size):
    return pl.ds(pl.multiple_of(v, m), size)


def backward_kernel(
    scale, feat_hbm, cot_hbm, w_hbm, ig_hbm, kg_hbm,
    ext, stack, raw, flat, wv, wt, part, first, second, low, third, fin, prod, other, across, ig,
    load_sem, halo_send, halo_recv, feat_send, feat_recv, sum_send, sum_recv, ig_send, ig_recv,
):
    lon = lax.axis_index("lon")
    ch = lax.axis_index("ch")
    lons = Y * Z * X
    y, z, x = lon // (Z * X), lax.rem(lon // X, Z), lax.rem(lon, X)
    xh, core = ch // 2, lax.rem(ch, 2)
    cols = feat_hbm.shape[0]
    in_rows = feat_hbm.shape[1]
    out_rows = cot_hbm.shape[2]
    taps = 9 * out_rows
    rows = taps // 4
    here = (y, z)

    def at(dy, dz, dx):
        return (mod4(y + dy) * (Z * X) + mod4(z + dz) * X + lax.rem(x + dx, X), ch)

    hops = [(d, 0, 0) for d in (1, 2, 3)], [(0, d, 0) for d in (1, 2, 3)]
    right = (lax.rem(lon + 1, lons), ch)
    left = (lax.rem(lon + lons - 1, lons), ch)
    mate = (lon, xh * 2 + 1 - core)
    far = (lon, (1 - xh) * 2 + core)

    load_w = pltpu.make_async_copy(w_hbm, wv.at[pl.ds(0, 3 * taps)], load_sem.at[0])
    load_f = pltpu.make_async_copy(feat_hbm, raw.at[ch], load_sem.at[1])
    loads = [
        pltpu.make_async_copy(cot_hbm.at[k], ext.at[pl.ds(BASES[k] + d, cols)], load_sem.at[2 + k])
        for k, d in enumerate(DILATIONS)
    ]
    for copy in loads:
        copy.start()
    load_f.start()
    load_w.start()

    barrier = pltpu.get_barrier_semaphore()
    peers = [at(*hop) for hop in hops[0] + hops[1] + [(0, 0, 1)]] + [right, left, mate, far]
    for peer in peers:
        pl.semaphore_signal(barrier, inc=1, device_id=peer, device_id_type=MESH)
    pl.semaphore_wait(barrier, len(peers))

    def remote(src, dst, send, recv, peer):
        return pltpu.make_async_remote_copy(
            src_ref=src, dst_ref=dst, send_sem=send, recv_sem=recv, device_id=peer, device_id_type=MESH
        )

    halos = []
    for k, d in enumerate(DILATIONS):
        to_right = remote(
            cot_hbm.at[k, pl.ds(cols - d, d)], ext.at[pl.ds(BASES[k], d)], halo_send.at[2 * k], halo_recv.at[2 * k], right
        )
        to_left = remote(
            cot_hbm.at[k, pl.ds(0, d)],
            ext.at[pl.ds(BASES[k] + d + cols, d)],
            halo_send.at[2 * k + 1],
            halo_recv.at[2 * k + 1],
            left,
        )
        to_right.start()
        to_left.start()
        halos.append((to_right, to_left))
    feat_mate = remote(feat_hbm, raw.at[ch], feat_send.at[0], feat_recv.at[0], mate)
    feat_far = remote(feat_hbm, raw.at[ch], feat_send.at[1], feat_recv.at[1], far)
    far_ch = (1 - xh) * 2 + core
    feat_on = remote(raw.at[far_ch], raw.at[far_ch], feat_send.at[2], feat_recv.at[2], mate)
    feat_mate.start()
    feat_far.start()

    lane = lax.broadcasted_iota(jnp.int32, (out_rows, 128), 1)

    def build(k):
        d, base = DILATIONS[k], BASES[k]

        def column(m, carry):
            for lon_tap in range(3):
                v = ext[base + d + m - d * (lon_tap - 1)].astype(jnp.float32)
                for lat_tap in range(3):
                    if lat_tap == 0:
                        moved = jnp.where(lane < 128 - d, pltpu.roll(v, 128 - d, 1), 0.0)
                    elif lat_tap == 1:
                        moved = v
                    else:
                        moved = jnp.where(lane >= d, pltpu.roll(v, d, 1), 0.0)
                    row = k * taps + (lat_tap * 3 + lon_tap) * out_rows
                    stack[pl.ds(row, out_rows), aligned(m * 128, 128, 128)] = moved.astype(jnp.bfloat16)
            return carry

        lax.fori_loop(0, cols, column, 0)

    def flatten(pair):
        def column(m, carry):
            for jj in range(2):
                flat[pl.ds(jj * in_rows, in_rows), aligned(m * 128, 128, 128)] = raw[pair * 2 + jj, m]
            return carry

        lax.fori_loop(0, cols, column, 0)

    def rs1(e, h):
        out = []
        for d in range(3):
            there = mod4(here[h] + d + 1)
            slot = h * 3 + d
            out.append(
                remote(
                    part.at[e, aligned(there * rows, 8, rows), pl.ds(h * 256, 256)],
                    first.at[e, h, d],
                    sum_send.at[e, slot],
                    sum_recv.at[e, slot],
                    at(*hops[h][d]),
                )
            )
        return out

    def piece(h, q, base_row=0, base_col=0):
        return (
            aligned(base_row + here[h] * rows + (q // 2) * (rows // 2), 8, rows // 2),
            aligned(base_col + h * 256 + lax.rem(q, 2) * 128, 128, 128),
        )

    def rs2(e, h):
        out = []
        for d in range(3):
            q = mod4(here[1 - h] + d + 1)
            slot = 6 + h * 3 + d
            r, c = piece(h, q)
            out.append(
                remote(part.at[e, r, c], second.at[e, h, d], sum_send.at[e, slot], sum_recv.at[e, slot], at(*hops[1 - h][d]))
            )
        return out

    def swap(e, h):
        return remote(low.at[e, h], third.at[e, h], sum_send.at[e, 12 + h], sum_recv.at[e, 12 + h], at(0, 0, 1))

    def corner(e):
        pair = jnp.where(e < 3, xh, 1 - xh)
        return lax.rem(e, 3) * taps, pair * 512

    def ag2_local(e, h):
        r, c = piece(h, here[1 - h], *corner(e))
        return pltpu.make_async_copy(fin.at[e, h], kg_hbm.at[r, c], load_sem.at[5 + 2 * e + h])

    def ag2(e, h):
        r, c = piece(h, here[1 - h], *corner(e))
        return [
            remote(
                fin.at[e, h], kg_hbm.at[r, c], sum_send.at[e, 14 + h * 3 + d], sum_recv.at[e, 14 + h * 3 + d], at(*hops[1 - h][d])
            )
            for d in range(3)
        ]

    def ag1(e, h):
        base_row, base_col = corner(e)
        area = kg_hbm.at[
            aligned(base_row + here[h] * rows, 8, rows), aligned(base_col + h * 256, 128, 256)
        ]
        return [
            remote(area, area, sum_send.at[e, 20 + h * 3 + d], sum_recv.at[e, 20 + h * 3 + d], at(*hops[h][d]))
            for d in range(3)
        ]

    def do_chunk(e):
        k = lax.rem(e, 3)
        for h in range(2):
            part[e, :, pl.ds(h * 256, 256)] = lax.dot_general(
                stack[aligned(k * taps, 16, taps), :],
                flat[pl.ds(h * 256, 256), :],
                (((1,), (1,)), ((), ())),
                preferred_element_type=jnp.float32,
            )
            for copy in rs1(e, h):
                copy.start()

    def do_rs2(e):
        for h in range(2):
            for copy in rs1(e, h):
                copy.wait()

            def step(i, carry):
                r = aligned(i * 16, 16, 16)
                mine = aligned(here[h] * rows + i * 16, 8, 16)
                part[e, mine, pl.ds(h * 256, 256)] = (part[e, mine, pl.ds(h * 256, 256)] + first[e, h, 0, r, :]) + (
                    first[e, h, 1, r, :] + first[e, h, 2, r, :]
                )
                return carry

            lax.fori_loop(0, rows // 16, step, 0)
            for copy in rs2(e, h):
                copy.start()

    def do_swap(e):
        for h in range(2):
            for copy in rs2(e, h):
                copy.wait()
            r, c = piece(h, here[1 - h])
            low[e, h] = (part[e, r, c] + second[e, h, 0]) + (second[e, h, 1] + second[e, h, 2])
            swap(e, h).start()

    def do_ag2(e):
        for h in range(2):
            swap(e, h).wait()
            fin[e, h] = (low[e, h] + third[e, h]) * scale
            ag2_local(e, h).start()
            for copy in ag2(e, h):
                copy.start()

    def do_ag1(e):
        for h in range(2):
            ag2_local(e, h).wait()
            for copy in ag2(e, h):
                copy.wait()
            for copy in ag1(e, h):
                copy.start()

    def do_end(e):
        for h in range(2):
            for copy in ag1(e, h):
                copy.wait()

    def ig_block(g):
        chip = jnp.where(g < 2, 1 - xh, xh)
        who = jnp.where(lax.rem(g, 2) == 0, 1 - core, core)
        j = chip * 2 + who
        wt[...] = wv[:, aligned(j * in_rows, 128, in_rows)].T

        def tile(m, carry):
            res = jnp.dot(wt[...], stack[:, aligned(m * 256, 256, 256)], preferred_element_type=jnp.float32)
            prod[g, 2 * m] = res[:, :128]
            prod[g, 2 * m + 1] = res[:, 128:]
            return carry

        lax.fori_loop(0, cols // 2, tile, 0)

    def ig_mate(g):
        return remote(prod.at[2 * g], other.at[g], ig_send.at[g], ig_recv.at[g], mate)

    ig_far = remote(prod.at[1], across, ig_send.at[2], ig_recv.at[2], far)

    def add_other(g):
        def column(m, carry):
            prod[2 * g + 1, m] = prod[2 * g + 1, m] + other[g, m]
            return carry

        lax.fori_loop(0, cols, column, 0)

    pad = stack.shape[0] - 3 * taps
    stack[pl.ds(3 * taps, pad), :] = jnp.zeros((pad, stack.shape[1]), stack.dtype)
    wv[pl.ds(3 * taps, pad), :] = jnp.zeros((pad, wv.shape[1]), wv.dtype)

    def body(s, carry):
        for k in range(3):

            @pl.when(s == k)
            def _():
                loads[k].wait()
                for copy in halos[k]:
                    copy.wait()
                build(k)

        @pl.when(s == 0)
        def _():
            load_f.wait()
            feat_mate.wait()
            flatten(xh)

        @pl.when(s == 3)
        def _():
            feat_on.wait()
            flatten(1 - xh)

        @pl.when(s < CHUNKS)
        def _():
            do_chunk(s)

        @pl.when(s == 2)
        def _():
            feat_far.wait()
            feat_on.start()

        @pl.when((s >= 4) & (s < CHUNKS + 4))
        def _():
            do_ag1(s - 4)

        @pl.when((s >= 3) & (s < CHUNKS + 3))
        def _():
            do_ag2(s - 3)

        @pl.when((s >= 2) & (s < CHUNKS + 2))
        def _():
            do_swap(s - 2)

        @pl.when((s >= 1) & (s < CHUNKS + 1))
        def _():
            do_rs2(s - 1)

        @pl.when(s == 2)
        def _():
            load_w.wait()

        @pl.when((s >= 2) & (s < 6))
        def _():
            g = s - 2
            ig_block(g)

            @pl.when(g == 0)
            def _():
                ig_mate(0).start()

            @pl.when(g == 2)
            def _():
                ig_mate(1).start()

            @pl.when(g == 1)
            def _():
                ig_mate(0).wait()
                add_other(0)
                ig_far.start()

            @pl.when(g == 3)
            def _():
                ig_mate(1).wait()
                add_other(1)

        return carry

    lax.fori_loop(0, CHUNKS + 4, body, 0)
    ig_far.wait()

    def column(m, carry):
        ig[m] = (prod[3, m] + across[m]).astype(jnp.bfloat16)
        return carry

    lax.fori_loop(0, cols, column, 0)
    store = pltpu.make_async_copy(ig, ig_hbm, load_sem.at[0])
    store.start()

    def end(e, carry):
        do_end(e)
        return carry

    lax.fori_loop(0, CHUNKS, end, 0)
    store.wait()


def local(features, cotangent, weights):
    in_rows, _, cols, lats = features.shape
    out_rows, in_total = weights.shape[3:]
    cells = cols * lats
    taps = 9 * out_rows
    rows = taps // 4
    depth = -(-3 * taps // 256) * 256
    scale = 1.0 / math.sqrt(cells * lax.axis_size("lon"))
    f32, bf16 = jnp.float32, jnp.bfloat16
    anywhere = pl.BlockSpec(memory_space=pl.ANY)
    ig, kg = pl.pallas_call(
        functools.partial(backward_kernel, scale),
        out_shape=(
            jax.ShapeDtypeStruct((cols, in_rows, lats), bf16),
            jax.ShapeDtypeStruct((3 * taps, in_total), f32),
        ),
        in_specs=[anywhere] * 3,
        out_specs=(anywhere, anywhere),
        scratch_shapes=[
            pltpu.VMEM((126, out_rows, lats), bf16),
            pltpu.VMEM((depth, cells), bf16),
            pltpu.VMEM((4, cols, in_rows, lats), bf16),
            pltpu.VMEM((2 * in_rows, cells), bf16),
            pltpu.VMEM((depth, in_total), bf16),
            pltpu.VMEM((in_rows, depth), bf16),
            pltpu.VMEM((CHUNKS, taps, 512), f32),
            pltpu.VMEM((CHUNKS, 2, 3, rows, 256), f32),
            pltpu.VMEM((CHUNKS, 2, 3, rows // 2, 128), f32),
            pltpu.VMEM((CHUNKS, 2, rows // 2, 128), f32),
            pltpu.VMEM((CHUNKS, 2, rows // 2, 128), f32),
            pltpu.VMEM((CHUNKS, 2, rows // 2, 128), f32),
            pltpu.VMEM((4, cols, in_rows, lats), f32),
            pltpu.VMEM((2, cols, in_rows, lats), f32),
            pltpu.VMEM((cols, in_rows, lats), f32),
            pltpu.VMEM((cols, in_rows, lats), bf16),
            pltpu.SemaphoreType.DMA((5 + 2 * CHUNKS,)),
            pltpu.SemaphoreType.DMA((6,)),
            pltpu.SemaphoreType.DMA((6,)),
            pltpu.SemaphoreType.DMA((3,)),
            pltpu.SemaphoreType.DMA((3,)),
            pltpu.SemaphoreType.DMA((CHUNKS, 26)),
            pltpu.SemaphoreType.DMA((CHUNKS, 26)),
            pltpu.SemaphoreType.DMA((3,)),
            pltpu.SemaphoreType.DMA((3,)),
        ],
        compiler_params=pltpu.CompilerParams(
            collective_id=1, has_side_effects=True, vmem_limit_bytes=60 * 1024 * 1024
        ),
        name="backward",
    )(
        features.reshape(in_rows, cols, lats).transpose(1, 0, 2),
        cotangent.reshape(3, out_rows, cols, lats).transpose(0, 2, 1, 3),
        weights.reshape(3 * taps, in_total),
    )
    input_grad = ig.transpose(1, 0, 2).reshape(in_rows, 1, cols, lats)
    return (input_grad, kg.reshape(3, 3, 3, out_rows, in_total))


def solution(mesh):
    return jax.shard_map(
        local,
        mesh=mesh,
        in_specs=(
            P("ch", None, "lon", None),
            P(None, "ch", None, "lon", None),
            P(None, None, None, "ch", None),
        ),
        out_specs=(P("ch", None, "lon", None), P(None, None, None, "ch", None)),
        check_vma=False,
    )
```

```python
import functools
import math

import jax
import jax.numpy as jnp
from jax import lax
from jax.experimental import pallas as pl
from jax.experimental.pallas import tpu as pltpu
from jax.sharding import PartitionSpec as P

DILATIONS = (6, 12, 18)
BASES = (0, 48, 108)
MESH = pl.DeviceIdType.MESH
Y, Z, X = 4, 4, 2
CHUNKS = 6
LAG = (1, 2, 3, 4)


def mod4(v):
    return lax.rem(v, 4)


def aligned(v, m, size):
    return pl.ds(pl.multiple_of(v, m), size)


def backward_kernel(
    scale, feat_hbm, cot_hbm, w_hbm, ig_hbm, kg_hbm,
    ext, stack, raw, flat, wv, wt, part, first, second, low, third, fin, prod, other, across, ig,
    load_sem, halo_send, halo_recv, feat_send, feat_recv, sum_send, sum_recv, ig_send, ig_recv,
):
    lon = lax.axis_index("lon")
    ch = lax.axis_index("ch")
    lons = Y * Z * X
    y, z, x = lon // (Z * X), lax.rem(lon // X, Z), lax.rem(lon, X)
    xh, core = ch // 2, lax.rem(ch, 2)
    cols = feat_hbm.shape[0]
    in_rows = feat_hbm.shape[1]
    out_rows = cot_hbm.shape[2]
    taps = 9 * out_rows
    rows = taps // 4
    here = (y, z)

    def at(dy, dz, dx):
        return (mod4(y + dy) * (Z * X) + mod4(z + dz) * X + lax.rem(x + dx, X), ch)

    hops = [(d, 0, 0) for d in (1, 2, 3)], [(0, d, 0) for d in (1, 2, 3)]
    twin = at(0, 0, 1)
    pair = lon - x
    mate = (lon, xh * 2 + 1 - core)
    far = (pair + 1 - x, (1 - xh) * 2 + core)
    outer = [(lax.rem(pair + step, lons), ch) for step in (lons - 2, lons - 1, 2, 3)]
    halo_to = [(lax.rem(pair + lons - 2 + 4 * x + i, lons), ch) for i in range(2)]

    load_w = pltpu.make_async_copy(w_hbm, wv.at[pl.ds(0, 3 * taps)], load_sem.at[0])
    load_f = pltpu.make_async_copy(feat_hbm, raw.at[core], load_sem.at[1])
    loads = [
        pltpu.make_async_copy(cot_hbm.at[k], ext.at[pl.ds(BASES[k] + d + x * cols, cols)], load_sem.at[2 + k])
        for k, d in enumerate(DILATIONS)
    ]
    for copy in loads:
        copy.start()
    load_f.start()
    load_w.start()

    barrier = pltpu.get_barrier_semaphore()
    peers = [at(*hop) for hop in hops[0] + hops[1]] + [twin, mate, far] + outer
    for peer in peers:
        pl.semaphore_signal(barrier, inc=1, device_id=peer, device_id_type=MESH)
    pl.semaphore_wait(barrier, len(peers))

    def remote(src, dst, send, recv, peer):
        return pltpu.make_async_remote_copy(
            src_ref=src, dst_ref=dst, send_sem=send, recv_sem=recv, device_id=peer, device_id_type=MESH
        )

    inputs = []
    for k, d in enumerate(DILATIONS):
        base = BASES[k]
        mine = remote(
            cot_hbm.at[k], ext.at[pl.ds(base + d + x * cols, cols)], halo_send.at[3 * k], halo_recv.at[3 * k], twin
        )
        edges = [
            remote(
                cot_hbm.at[k, pl.ds(x * (cols - d), d)],
                ext.at[pl.ds(base + (1 - x) * (2 * cols + d), d)],
                halo_send.at[3 * k + 1 + i],
                halo_recv.at[3 * k + 1 + (1 - x)],
                halo_to[i],
            )
            for i in range(2)
        ]
        for copy in edges + [mine]:
            copy.start()
        before = ext.at[pl.ds(base, d)]
        after = ext.at[pl.ds(base + 2 * cols + d, d)]
        arrivals = [
            remote(before, before, halo_send.at[3 * k + 1], halo_recv.at[3 * k + 1], halo_to[0]),
            remote(after, after, halo_send.at[3 * k + 1], halo_recv.at[3 * k + 2], halo_to[0]),
        ]
        inputs.append((mine, edges, arrivals))
    feat_mate = remote(feat_hbm, raw.at[core], feat_send.at[0], feat_recv.at[0], mate)
    feat_far = remote(feat_hbm, raw.at[2 + core], feat_send.at[1], feat_recv.at[1], far)
    feat_on = remote(raw.at[2 + core], raw.at[2 + core], feat_send.at[2], feat_recv.at[2], mate)
    feat_mate.start()
    feat_far.start()

    lane = lax.broadcasted_iota(jnp.int32, (out_rows, 128), 1)

    def build(k, side):
        d, base = DILATIONS[k], BASES[k]

        def column(m, carry):
            for lon_tap in range(3):
                v = ext[base + d + side * cols + m - d * (lon_tap - 1)].astype(jnp.float32)
                for lat_tap in range(3):
                    if lat_tap == 0:
                        moved = jnp.where(lane < 128 - d, pltpu.roll(v, 128 - d, 1), 0.0)
                    elif lat_tap == 1:
                        moved = v
                    else:
                        moved = jnp.where(lane >= d, pltpu.roll(v, d, 1), 0.0)
                    row = k * taps + (lat_tap * 3 + lon_tap) * out_rows
                    stack[pl.ds(row, out_rows), aligned(m * 128, 128, 128)] = moved.astype(jnp.bfloat16)
            return carry

        lax.fori_loop(0, cols, column, 0)

    def flatten(chip):
        def column(m, carry):
            for jj in range(2):
                flat[pl.ds(jj * in_rows, in_rows), aligned(m * 128, 128, 128)] = raw[chip * 2 + jj, m]
            return carry

        lax.fori_loop(0, cols, column, 0)

    def rs1(e, h):
        out = []
        for d in range(3):
            there = mod4(here[h] + d + 1)
            slot = h * 3 + d
            out.append(
                remote(
                    part.at[e, aligned(there * rows, 8, rows), pl.ds(h * 256, 256)],
                    first.at[e, h, d],
                    sum_send.at[e, slot],
                    sum_recv.at[e, slot],
                    at(*hops[h][d]),
                )
            )
        return out

    def piece(h, q, base_row=0, base_col=0):
        return (
            aligned(base_row + here[h] * rows + (q // 2) * (rows // 2), 8, rows // 2),
            aligned(base_col + h * 256 + lax.rem(q, 2) * 128, 128, 128),
        )

    def rs2(e, h):
        out = []
        for d in range(3):
            q = mod4(here[1 - h] + d + 1)
            slot = 6 + h * 3 + d
            r, c = piece(h, q)
            out.append(
                remote(part.at[e, r, c], second.at[e, h, d], sum_send.at[e, slot], sum_recv.at[e, slot], at(*hops[1 - h][d]))
            )
        return out

    def swap(e, h):
        return remote(low.at[e, h], third.at[e, h], sum_send.at[e, 12 + h], sum_recv.at[e, 12 + h], at(0, 0, 1))

    def corner(e):
        chip = jnp.where(e < 3, xh, 1 - xh)
        return lax.rem(e, 3) * taps, chip * 512

    def ag2_local(e, h):
        r, c = piece(h, here[1 - h], *corner(e))
        return pltpu.make_async_copy(fin.at[e, h], kg_hbm.at[r, c], load_sem.at[5 + 2 * e + h])

    def ag2(e, h):
        r, c = piece(h, here[1 - h], *corner(e))
        return [
            remote(
                fin.at[e, h], kg_hbm.at[r, c], sum_send.at[e, 14 + h * 3 + d], sum_recv.at[e, 14 + h * 3 + d], at(*hops[1 - h][d])
            )
            for d in range(3)
        ]

    def ag1(e, h):
        base_row, base_col = corner(e)
        area = kg_hbm.at[
            aligned(base_row + here[h] * rows, 8, rows), aligned(base_col + h * 256, 128, 256)
        ]
        return [
            remote(area, area, sum_send.at[e, 20 + h * 3 + d], sum_recv.at[e, 20 + h * 3 + d], at(*hops[h][d]))
            for d in range(3)
        ]

    def do_chunk(e):
        k = lax.rem(e, 3)
        for h in range(2):
            part[e, :, pl.ds(h * 256, 256)] = lax.dot_general(
                stack[aligned(k * taps, 16, taps), :],
                flat[pl.ds(h * 256, 256), :],
                (((1,), (1,)), ((), ())),
                preferred_element_type=jnp.float32,
            )
            for copy in rs1(e, h):
                copy.start()

    def do_rs2(e):
        for h in range(2):
            for copy in rs1(e, h):
                copy.wait()

            def step(i, carry):
                r = aligned(i * 16, 16, 16)
                mine = aligned(here[h] * rows + i * 16, 8, 16)
                part[e, mine, pl.ds(h * 256, 256)] = (part[e, mine, pl.ds(h * 256, 256)] + first[e, h, 0, r, :]) + (
                    first[e, h, 1, r, :] + first[e, h, 2, r, :]
                )
                return carry

            lax.fori_loop(0, rows // 16, step, 0)
            for copy in rs2(e, h):
                copy.start()

    def do_swap(e):
        for h in range(2):
            for copy in rs2(e, h):
                copy.wait()
            r, c = piece(h, here[1 - h])
            low[e, h] = (part[e, r, c] + second[e, h, 0]) + (second[e, h, 1] + second[e, h, 2])
            swap(e, h).start()

    def do_ag2(e):
        for h in range(2):
            swap(e, h).wait()
            fin[e, h] = (low[e, h] + third[e, h]) * scale
            ag2_local(e, h).start()
            for copy in ag2(e, h):
                copy.start()

    def do_ag1(e):
        for h in range(2):
            ag2_local(e, h).wait()
            for copy in ag2(e, h):
                copy.wait()
            for copy in ag1(e, h):
                copy.start()

    def do_end(e):
        for h in range(2):
            for copy in ag1(e, h):
                copy.wait()

    def ig_block(g):
        chip = jnp.where(g < 2, xh, 1 - xh)
        who = jnp.where(lax.rem(g, 2) == 0, 1 - core, core)
        j = chip * 2 + who
        wt[...] = wv[:, aligned(j * in_rows, 128, in_rows)].T

        def tile(m, carry):
            res = jnp.dot(wt[...], stack[:, aligned(m * 256, 256, 256)], preferred_element_type=jnp.float32)
            prod[g, 2 * m] = res[:, :128]
            prod[g, 2 * m + 1] = res[:, 128:]
            return carry

        lax.fori_loop(0, cols // 2, tile, 0)

    def ig_mate(g):
        return remote(prod.at[2 * g], other.at[g], ig_send.at[g], ig_recv.at[g], mate)

    ig_far = remote(prod.at[3], across, ig_send.at[2], ig_recv.at[2], far)

    def add_other(g):
        def column(m, carry):
            prod[2 * g + 1, m] = prod[2 * g + 1, m] + other[g, m]
            return carry

        lax.fori_loop(0, cols, column, 0)

    pad = stack.shape[0] - 3 * taps
    stack[pl.ds(3 * taps, pad), :] = jnp.zeros((pad, stack.shape[1]), stack.dtype)
    wv[pl.ds(3 * taps, pad), :] = jnp.zeros((pad, wv.shape[1]), wv.dtype)

    def body(s, carry):
        for k in range(3):

            @pl.when(s == k)
            def _():
                mine, edges, arrivals = inputs[k]
                loads[k].wait()
                mine.wait_recv()
                for copy in arrivals:
                    copy.wait_recv()
                build(k, x)

            @pl.when(s == 3 + k)
            def _():
                build(k, 1 - x)

        @pl.when(s == 0)
        def _():
            load_f.wait()
            feat_mate.wait()
            flatten(0)

        @pl.when(s == 3)
        def _():
            feat_on.wait()
            flatten(1)

        @pl.when(s < CHUNKS)
        def _():
            do_chunk(s)

        @pl.when(s == 2)
        def _():
            feat_far.wait()
            feat_on.start()
            load_w.wait()
            ig_block(0)
            ig_mate(0).start()
            ig_block(1)

        @pl.when(s == 5)
        def _():
            ig_block(2)
            ig_mate(1).start()
            ig_block(3)

        @pl.when(s == 6)
        def _():
            ig_mate(1).wait()
            add_other(1)
            ig_far.start()
            ig_mate(0).wait()
            add_other(0)

        for lag, work in zip(LAG[::-1], (do_ag1, do_ag2, do_swap, do_rs2)):

            @pl.when((s >= lag) & (s < CHUNKS + lag))
            def _():
                work(s - lag)

        return carry

    lax.fori_loop(0, CHUNKS + LAG[3], body, 0)
    ig_far.wait()

    def column(m, carry):
        ig[m] = (prod[1, m] + across[m]).astype(jnp.bfloat16)
        return carry

    lax.fori_loop(0, cols, column, 0)
    store = pltpu.make_async_copy(ig, ig_hbm, load_sem.at[0])
    store.start()
    for mine, edges, _ in inputs:
        mine.wait_send()
        for copy in edges:
            copy.wait_send()

    def end(e, carry):
        do_end(e)
        return carry

    lax.fori_loop(0, CHUNKS, end, 0)
    store.wait()


def local(features, cotangent, weights):
    in_rows, _, cols, lats = features.shape
    out_rows, in_total = weights.shape[3:]
    cells = cols * lats
    taps = 9 * out_rows
    rows = taps // 4
    depth = -(-3 * taps // 256) * 256
    scale = 1.0 / math.sqrt(cells * lax.axis_size("lon"))
    f32, bf16 = jnp.float32, jnp.bfloat16
    anywhere = pl.BlockSpec(memory_space=pl.ANY)
    ig, kg = pl.pallas_call(
        functools.partial(backward_kernel, scale),
        out_shape=(
            jax.ShapeDtypeStruct((cols, in_rows, lats), bf16),
            jax.ShapeDtypeStruct((3 * taps, in_total), f32),
        ),
        in_specs=[anywhere] * 3,
        out_specs=(anywhere, anywhere),
        scratch_shapes=[
            pltpu.VMEM((180, out_rows, lats), bf16),
            pltpu.VMEM((depth, cells), bf16),
            pltpu.VMEM((4, cols, in_rows, lats), bf16),
            pltpu.VMEM((2 * in_rows, cells), bf16),
            pltpu.VMEM((depth, in_total), bf16),
            pltpu.VMEM((in_rows, depth), bf16),
            pltpu.VMEM((CHUNKS, taps, 512), f32),
            pltpu.VMEM((CHUNKS, 2, 3, rows, 256), f32),
            pltpu.VMEM((CHUNKS, 2, 3, rows // 2, 128), f32),
            pltpu.VMEM((CHUNKS, 2, rows // 2, 128), f32),
            pltpu.VMEM((CHUNKS, 2, rows // 2, 128), f32),
            pltpu.VMEM((CHUNKS, 2, rows // 2, 128), f32),
            pltpu.VMEM((4, cols, in_rows, lats), f32),
            pltpu.VMEM((2, cols, in_rows, lats), f32),
            pltpu.VMEM((cols, in_rows, lats), f32),
            pltpu.VMEM((cols, in_rows, lats), bf16),
            pltpu.SemaphoreType.DMA((5 + 2 * CHUNKS,)),
            pltpu.SemaphoreType.DMA((9,)),
            pltpu.SemaphoreType.DMA((9,)),
            pltpu.SemaphoreType.DMA((3,)),
            pltpu.SemaphoreType.DMA((3,)),
            pltpu.SemaphoreType.DMA((CHUNKS, 26)),
            pltpu.SemaphoreType.DMA((CHUNKS, 26)),
            pltpu.SemaphoreType.DMA((3,)),
            pltpu.SemaphoreType.DMA((3,)),
        ],
        compiler_params=pltpu.CompilerParams(
            collective_id=1, has_side_effects=True, vmem_limit_bytes=60 * 1024 * 1024
        ),
        name="backward",
    )(
        features.reshape(in_rows, cols, lats).transpose(1, 0, 2),
        cotangent.reshape(3, out_rows, cols, lats).transpose(0, 2, 1, 3),
        weights.reshape(3 * taps, in_total),
    )
    input_grad = ig.transpose(1, 0, 2).reshape(in_rows, 1, cols, lats)
    return (input_grad, kg.reshape(3, 3, 3, out_rows, in_total))


def solution(mesh):
    return jax.shard_map(
        local,
        mesh=mesh,
        in_specs=(
            P("ch", None, "lon", None),
            P(None, "ch", None, "lon", None),
            P(None, None, None, "ch", None),
        ),
        out_specs=(P("ch", None, "lon", None), P(None, None, None, "ch", None)),
        check_vma=False,
    )
```

```python
import functools
import math

import jax
import jax.numpy as jnp
from jax import lax
from jax.experimental import pallas as pl
from jax.experimental.pallas import tpu as pltpu
from jax.sharding import PartitionSpec as P

DILATIONS = (6, 12, 18)
BASES = (0, 48, 108)
MESH = pl.DeviceIdType.MESH
Y, Z, X = 4, 4, 2
CHUNKS = 6
LAG = (1, 2, 3, 4, 5, 6)
GROUPS = 3


def mod4(v):
    return lax.rem(v, 4)


def aligned(v, m, size):
    return pl.ds(pl.multiple_of(v, m), size)


def backward_kernel(
    scale, feat_hbm, cot_hbm, w_hbm, ig_hbm, kg_hbm,
    ext, stack, raw, flat, wcol, wt, part, first, second, low, third, prod, other, across, ig,
    load_sem, halo_send, halo_recv, feat_send, feat_recv, sum_send, sum_recv, ig_send, ig_recv,
):
    lon = lax.axis_index("lon")
    ch = lax.axis_index("ch")
    lons = Y * Z * X
    y, z, x = lon // (Z * X), lax.rem(lon // X, Z), lax.rem(lon, X)
    xh, core = ch // 2, lax.rem(ch, 2)
    cols = feat_hbm.shape[0]
    in_rows = feat_hbm.shape[1]
    out_rows = cot_hbm.shape[2]
    taps = 9 * out_rows
    rows = taps // 4
    here = (y, z)

    def at(dy, dz, dx):
        return (mod4(y + dy) * (Z * X) + mod4(z + dz) * X + lax.rem(x + dx, X), ch)

    hops = [(d, 0, 0) for d in (1, 2, 3)], [(0, d, 0) for d in (1, 2, 3)]
    twin = at(0, 0, 1)
    pair = lon - x
    mate = (lon, xh * 2 + 1 - core)
    far = (pair + 1 - x, (1 - xh) * 2 + core)
    outer = [(lax.rem(pair + step, lons), ch) for step in (lons - 2, lons - 1, 2, 3)]
    halo_to = [(lax.rem(pair + lons - 2 + 4 * x + i, lons), ch) for i in range(2)]

    def load_w(chip, who):
        columns = aligned((chip * 2 + who) * in_rows, 128, in_rows)
        return pltpu.make_async_copy(w_hbm.at[:, columns], wcol.at[pl.ds(0, 3 * taps)], load_sem.at[0])

    load_f = pltpu.make_async_copy(feat_hbm, raw.at[core], load_sem.at[1])
    loads = [
        pltpu.make_async_copy(cot_hbm.at[k], ext.at[pl.ds(BASES[k] + d + x * cols, cols)], load_sem.at[2 + k])
        for k, d in enumerate(DILATIONS)
    ]
    for copy in loads:
        copy.start()
    load_f.start()
    load_w(1 - xh, 1 - core).start()

    barrier = pltpu.get_barrier_semaphore()
    peers = [at(*hop) for hop in hops[0] + hops[1]] + [twin, mate, far] + outer
    for peer in peers:
        pl.semaphore_signal(barrier, inc=1, device_id=peer, device_id_type=MESH)
    pl.semaphore_wait(barrier, len(peers))

    def remote(src, dst, send, recv, peer):
        return pltpu.make_async_remote_copy(
            src_ref=src, dst_ref=dst, send_sem=send, recv_sem=recv, device_id=peer, device_id_type=MESH
        )

    inputs = []
    for k, d in enumerate(DILATIONS):
        base = BASES[k]
        mine = remote(
            cot_hbm.at[k], ext.at[pl.ds(base + d + x * cols, cols)], halo_send.at[3 * k], halo_recv.at[3 * k], twin
        )
        edges = [
            remote(
                cot_hbm.at[k, pl.ds(x * (cols - d), d)],
                ext.at[pl.ds(base + (1 - x) * (2 * cols + d), d)],
                halo_send.at[3 * k + 1 + i],
                halo_recv.at[3 * k + 1 + (1 - x)],
                halo_to[i],
            )
            for i in range(2)
        ]
        for copy in edges + [mine]:
            copy.start()
        before = ext.at[pl.ds(base, d)]
        after = ext.at[pl.ds(base + 2 * cols + d, d)]
        arrivals = [
            remote(before, before, halo_send.at[3 * k + 1], halo_recv.at[3 * k + 1], halo_to[0]),
            remote(after, after, halo_send.at[3 * k + 1], halo_recv.at[3 * k + 2], halo_to[0]),
        ]
        inputs.append((mine, edges, arrivals))
    feat_mate = remote(feat_hbm, raw.at[core], feat_send.at[0], feat_recv.at[0], mate)
    feat_far = remote(feat_hbm, raw.at[2 + core], feat_send.at[1], feat_recv.at[1], far)
    feat_on = remote(raw.at[2 + core], raw.at[2 + core], feat_send.at[2], feat_recv.at[2], mate)
    feat_mate.start()
    feat_far.start()

    lane = lax.broadcasted_iota(jnp.int32, (out_rows, 128), 1)

    def build(k, side, slot):
        d, base = DILATIONS[k], BASES[k]

        def column(m, carry):
            for lon_tap in range(3):
                v = ext[base + d + side * cols + m - d * (lon_tap - 1)].astype(jnp.float32)
                for lat_tap in range(3):
                    if lat_tap == 0:
                        moved = jnp.where(lane < 128 - d, pltpu.roll(v, 128 - d, 1), 0.0)
                    elif lat_tap == 1:
                        moved = v
                    else:
                        moved = jnp.where(lane >= d, pltpu.roll(v, d, 1), 0.0)
                    row = slot * taps + (lat_tap * 3 + lon_tap) * out_rows
                    stack[pl.ds(row, out_rows), aligned(m * 128, 128, 128)] = moved.astype(jnp.bfloat16)
            return carry

        lax.fori_loop(0, cols, column, 0)

    def flatten(chip):
        def column(m, carry):
            for jj in range(2):
                flat[pl.ds(jj * in_rows, in_rows), aligned(m * 128, 128, 128)] = raw[chip * 2 + jj, m]
            return carry

        lax.fori_loop(0, cols, column, 0)

    def order(e):
        far_side = (e >= 2) & (e < 5)
        return far_side, jnp.where(e < 2, e, jnp.where(far_side, e - 2, 2))

    def tile(h, block, sub, e):
        return part.at[e, aligned(mod4(here[h] + block) * rows, 8, rows), pl.ds(h * 256 + sub * 128, 128)]

    def rs1(e, h):
        up, down = at(*hops[h][0]), at(*hops[h][2])

        def send(i, src, peer):
            return remote(src, first.at[e, h, i], sum_send.at[e, h * 6 + i], sum_recv.at[e, h * 6 + i], peer)

        through = [send(0, tile(h, 2, 0, e), up), send(1, tile(h, 2, 1, e), down)]
        alone = [send(2, tile(h, 1, 1, e), up), send(3, tile(h, 3, 0, e), down)]
        both = [send(4, tile(h, 1, 0, e), up), send(5, tile(h, 3, 1, e), down)]
        return through, alone, both

    def piece(h, q, base_row=0, base_col=0):
        return (
            aligned(base_row + here[h] * rows + (q // 2) * (rows // 2), 8, rows // 2),
            aligned(base_col + h * 256 + lax.rem(q, 2) * 128, 128, 128),
        )

    def rs2(e, h):
        out = []
        for d in range(3):
            q = mod4(here[1 - h] + d + 1)
            slot = 12 + h * 3 + d
            r, c = piece(h, q)
            out.append(
                remote(part.at[e, r, c], second.at[e, h, d], sum_send.at[e, slot], sum_recv.at[e, slot], at(*hops[1 - h][d]))
            )
        return out

    def swap(e, h):
        return remote(low.at[e, h], third.at[e, h], sum_send.at[e, 18 + h], sum_recv.at[e, 18 + h], at(0, 0, 1))

    def corner(e):
        far_side, k = order(e)
        return k * taps, jnp.where(far_side, 1 - xh, xh) * 512

    def ag2_local(e, h):
        r, c = piece(h, here[1 - h], *corner(e))
        return pltpu.make_async_copy(low.at[e, h], kg_hbm.at[r, c], load_sem.at[5 + 2 * e + h])

    def ag2(e, h):
        r, c = piece(h, here[1 - h], *corner(e))
        return [
            remote(
                low.at[e, h], kg_hbm.at[r, c], sum_send.at[e, 20 + h * 3 + d], sum_recv.at[e, 20 + h * 3 + d], at(*hops[1 - h][d])
            )
            for d in range(3)
        ]

    def ag1(e, h):
        base_row, base_col = corner(e)
        up, down = at(*hops[h][0]), at(*hops[h][2])

        def send(i, block, sub, width, peer):
            area = kg_hbm.at[
                aligned(base_row + mod4(here[h] + block) * rows, 8, rows),
                aligned(base_col + h * 256 + sub * 128, 128, width),
            ]
            return remote(area, area, sum_send.at[e, 26 + h * 4 + i], sum_recv.at[e, 26 + h * 4 + i], peer)

        near = [send(0, 0, 0, 256, up), send(1, 0, 0, 256, down)]
        onward = [send(2, 3, 0, 128, up), send(3, 1, 1, 128, down)]
        return near, onward

    def do_chunk(e):
        far_side, k = order(e)
        slot = jnp.where(far_side, k, 3)
        for h in range(2):
            part[e, :, pl.ds(h * 256, 256)] = lax.dot_general(
                stack[aligned(slot * taps, 16, taps), :],
                flat[pl.ds(h * 256, 256), :],
                (((1,), (1,)), ((), ())),
                preferred_element_type=jnp.float32,
            )
            through, alone, _ = rs1(e, h)
            for copy in through + alone:
                copy.start()

    def do_rs1(e):
        for h in range(2):
            through, _, both = rs1(e, h)
            for i in range(2):
                through[i].wait()
                block, cols_at = (1, 3)[i], pl.ds(h * 256 + i * 128, 128)

                def step(n, carry):
                    r = aligned(mod4(here[h] + block) * rows + n * 16, 8, 16)
                    part[e, r, cols_at] = part[e, r, cols_at] + first[e, h, i, aligned(n * 16, 16, 16), :]
                    return carry

                lax.fori_loop(0, rows // 16, step, 0)
                both[i].start()

    def do_rs2(e):
        for h in range(2):
            _, alone, both = rs1(e, h)
            for copy in alone + both:
                copy.wait()

            def step(n, carry):
                r = aligned(n * 16, 16, 16)
                mine = aligned(here[h] * rows + n * 16, 8, 16)
                for sub, (a, b) in enumerate(((3, 4), (2, 5))):
                    c = pl.ds(h * 256 + sub * 128, 128)
                    part[e, mine, c] = part[e, mine, c] + (first[e, h, a, r, :] + first[e, h, b, r, :])
                return carry

            lax.fori_loop(0, rows // 16, step, 0)
            for copy in rs2(e, h):
                copy.start()

    def do_swap(e):
        for h in range(2):
            for copy in rs2(e, h):
                copy.wait()
            r, c = piece(h, here[1 - h])
            low[e, h] = (part[e, r, c] + second[e, h, 0]) + (second[e, h, 1] + second[e, h, 2])
            swap(e, h).start()

    def do_ag2(e):
        for h in range(2):
            swap(e, h).wait()
            low[e, h] = (low[e, h] + third[e, h]) * scale
            ag2_local(e, h).start()
            for copy in ag2(e, h):
                copy.start()

    def do_ag1(e):
        for h in range(2):
            ag2_local(e, h).wait()
            for copy in ag2(e, h):
                copy.wait()
            for copy in ag1(e, h)[0]:
                copy.start()

    def do_onward(e):
        for h in range(2):
            near, onward = ag1(e, h)
            near[1].wait_send()
            near[0].wait()
            onward[0].start()
            near[1].wait_recv()
            onward[1].start()

    def do_end(e):
        for h in range(2):
            for copy in ag1(e, h)[1]:
                copy.wait()

    wide = cols // GROUPS

    def turn(slot):
        wt[slot] = wcol[...].T

    def ig_group(slot, dst, q):
        def tile_of(i, carry):
            m = q * (wide // 2) + i
            res = jnp.dot(
                wt[slot], stack[pl.ds(0, wt.shape[2]), aligned(m * 256, 256, 256)], preferred_element_type=jnp.float32
            )
            prod[dst, 2 * m] = res[:, :128]
            prod[dst, 2 * m + 1] = res[:, 128:]
            return carry

        lax.fori_loop(0, wide // 2, tile_of, 0)

    def ig_mate(part_of, q):
        group = pl.ds(q * wide, wide)
        slot = part_of * GROUPS + q
        return remote(prod.at[0, group], other.at[part_of, group], ig_send.at[slot], ig_recv.at[slot], mate)

    def ig_far(q):
        group = pl.ds(q * wide, wide)
        slot = 2 * GROUPS + q
        return remote(prod.at[1, group], across.at[group], ig_send.at[slot], ig_recv.at[slot], far)

    def finish_far(q):
        ig_mate(1, q).wait()

        def column(i, carry):
            m = q * wide + i
            prod[1, m] = prod[1, m] + other[1, m]
            return carry

        lax.fori_loop(0, wide, column, 0)
        ig_far(q).start()

    def far_group(q, carry):
        ig_group(0, 0, q)
        ig_mate(1, q).start()
        ig_group(1, 1, q)

        @pl.when(q > 0)
        def _():
            finish_far(q - 1)

        return carry

    pad = wcol.shape[0] - 3 * taps
    wcol[pl.ds(3 * taps, pad), :] = jnp.zeros((pad, wcol.shape[1]), wcol.dtype)
    load_w(1 - xh, 1 - core).wait()
    turn(0)
    load_w(1 - xh, core).start()
    load_w(1 - xh, core).wait()
    turn(1)
    load_w(xh, 1 - core).start()

    def arrived(k):
        mine, edges, arrivals = inputs[k]
        loads[k].wait()
        mine.wait_recv()
        for copy in arrivals:
            copy.wait_recv()

    def body(s, carry):
        @pl.when(s == 0)
        def _():
            load_f.wait()
            feat_mate.wait()
            flatten(0)
            arrived(0)
            build(0, x, 3)

        @pl.when(s == 1)
        def _():
            arrived(1)
            build(1, x, 3)

        @pl.when(s == 2)
        def _():
            feat_far.wait()
            feat_on.start()
            build(0, 1 - x, 0)
            feat_on.wait()
            flatten(1)

        @pl.when(s == 3)
        def _():
            build(1, 1 - x, 1)

        @pl.when(s == 4)
        def _():
            arrived(2)
            build(2, 1 - x, 2)

        @pl.when(s == 5)
        def _():
            flatten(0)
            build(2, x, 3)

        @pl.when(s < CHUNKS)
        def _():
            do_chunk(s)

        @pl.when(s == 4)
        def _():
            lax.fori_loop(0, GROUPS, far_group, 0)
            finish_far(GROUPS - 1)

        @pl.when(s == 6)
        def _():
            load_w(xh, 1 - core).wait()
            turn(0)
            load_w(xh, core).start()
            for k in range(3):
                build(k, x, k)
            load_w(xh, core).wait()
            turn(1)

        @pl.when((s >= 7) & (s < 7 + GROUPS))
        def _():
            q = s - 7
            ig_group(0, 0, q)
            ig_mate(0, q).start()
            ig_group(1, 2, q)

        for lag, work in zip(LAG[::-1], (do_onward, do_ag1, do_ag2, do_swap, do_rs2, do_rs1)):

            @pl.when((s >= lag) & (s < CHUNKS + lag))
            def _():
                work(s - lag)

        return carry

    lax.fori_loop(0, CHUNKS + LAG[-1], body, 0)

    def last(q, carry):
        ig_mate(0, q).wait()
        ig_far(q).wait()

        def column(i, inner):
            m = q * wide + i
            ig[m] = (prod[2, m] + other[0, m] + across[m]).astype(jnp.bfloat16)
            return inner

        lax.fori_loop(0, wide, column, 0)
        return carry

    lax.fori_loop(0, GROUPS, last, 0)
    store = pltpu.make_async_copy(ig, ig_hbm, load_sem.at[0])
    store.start()
    for mine, edges, _ in inputs:
        mine.wait_send()
        for copy in edges:
            copy.wait_send()

    def end(e, carry):
        do_end(e)
        return carry

    lax.fori_loop(0, CHUNKS, end, 0)
    store.wait()


def local(features, cotangent, weights):
    in_rows, _, cols, lats = features.shape
    out_rows, in_total = weights.shape[3:]
    cells = cols * lats
    taps = 9 * out_rows
    rows = taps // 4
    depth = -(-3 * taps // 256) * 256
    scale = 1.0 / math.sqrt(cells * lax.axis_size("lon"))
    f32, bf16 = jnp.float32, jnp.bfloat16
    anywhere = pl.BlockSpec(memory_space=pl.ANY)
    ig, kg = pl.pallas_call(
        functools.partial(backward_kernel, scale),
        out_shape=(
            jax.ShapeDtypeStruct((cols, in_rows, lats), bf16),
            jax.ShapeDtypeStruct((3 * taps, in_total), f32),
        ),
        in_specs=[anywhere] * 3,
        out_specs=(anywhere, anywhere),
        scratch_shapes=[
            pltpu.VMEM((180, out_rows, lats), bf16),
            pltpu.VMEM((4 * taps, cells), bf16),
            pltpu.VMEM((4, cols, in_rows, lats), bf16),
            pltpu.VMEM((2 * in_rows, cells), bf16),
            pltpu.VMEM((depth, in_rows), bf16),
            pltpu.VMEM((2, in_rows, depth), bf16),
            pltpu.VMEM((CHUNKS, taps, 512), f32),
            pltpu.VMEM((CHUNKS, 2, 6, rows, 128), f32),
            pltpu.VMEM((CHUNKS, 2, 3, rows // 2, 128), f32),
            pltpu.VMEM((CHUNKS, 2, rows // 2, 128), f32),
            pltpu.VMEM((CHUNKS, 2, rows // 2, 128), f32),
            pltpu.VMEM((3, cols, in_rows, lats), f32),
            pltpu.VMEM((2, cols, in_rows, lats), f32),
            pltpu.VMEM((cols, in_rows, lats), f32),
            pltpu.VMEM((cols, in_rows, lats), bf16),
            pltpu.SemaphoreType.DMA((5 + 2 * CHUNKS,)),
            pltpu.SemaphoreType.DMA((9,)),
            pltpu.SemaphoreType.DMA((9,)),
            pltpu.SemaphoreType.DMA((3,)),
            pltpu.SemaphoreType.DMA((3,)),
            pltpu.SemaphoreType.DMA((CHUNKS, 34)),
            pltpu.SemaphoreType.DMA((CHUNKS, 34)),
            pltpu.SemaphoreType.DMA((3 * GROUPS,)),
            pltpu.SemaphoreType.DMA((3 * GROUPS,)),
        ],
        compiler_params=pltpu.CompilerParams(
            collective_id=1, has_side_effects=True, vmem_limit_bytes=52 * 1024 * 1024
        ),
        name="backward",
    )(
        features.reshape(in_rows, cols, lats).transpose(1, 0, 2),
        cotangent.reshape(3, out_rows, cols, lats).transpose(0, 2, 1, 3),
        weights.reshape(3 * taps, in_total),
    )
    input_grad = ig.transpose(1, 0, 2).reshape(in_rows, 1, cols, lats)
    return (input_grad, kg.reshape(3, 3, 3, out_rows, in_total))


def solution(mesh):
    return jax.shard_map(
        local,
        mesh=mesh,
        in_specs=(
            P("ch", None, "lon", None),
            P(None, "ch", None, "lon", None),
            P(None, None, None, "ch", None),
        ),
        out_specs=(P("ch", None, "lon", None), P(None, None, None, "ch", None)),
        check_vma=False,
    )
```

```python
import functools
import math

import jax
import jax.numpy as jnp
from jax import lax
from jax.experimental import pallas as pl
from jax.experimental.pallas import tpu as pltpu
from jax.sharding import PartitionSpec as P

DILATIONS = (6, 12, 18)
BASES = (0, 48, 108)
MESH = pl.DeviceIdType.MESH
Y, Z, X = 4, 4, 2
CHUNKS = 6
LAG = (1, 2, 3, 4, 5, 6)
GROUPS = 3


def mod4(v):
    return lax.rem(v, 4)


def aligned(v, m, size):
    return pl.ds(pl.multiple_of(v, m), size)


def backward_kernel(
    scale, feat_hbm, cot_hbm, w_hbm, ig_hbm, kg_hbm,
    ext, stack, raw, flat, wcol, wt, part, first, second, low, third, prod, other, across, ig,
    load_sem, halo_send, halo_recv, feat_send, feat_recv, sum_send, sum_recv, ig_send, ig_recv,
):
    lon = lax.axis_index("lon")
    ch = lax.axis_index("ch")
    lons = Y * Z * X
    y, z, x = lon // (Z * X), lax.rem(lon // X, Z), lax.rem(lon, X)
    xh, core = ch // 2, lax.rem(ch, 2)
    cols = feat_hbm.shape[0]
    in_rows = feat_hbm.shape[1]
    out_rows = cot_hbm.shape[2]
    taps = 9 * out_rows
    rows = taps // 4
    here = (y, z)

    def at(dy, dz, dx):
        return (mod4(y + dy) * (Z * X) + mod4(z + dz) * X + lax.rem(x + dx, X), ch)

    hops = [(d, 0, 0) for d in (1, 2, 3)], [(0, d, 0) for d in (1, 2, 3)]
    twin = at(0, 0, 1)
    pair = lon - x
    mate = (lon, xh * 2 + 1 - core)
    far = (pair + 1 - x, (1 - xh) * 2 + core)
    outer = [(lax.rem(pair + step, lons), ch) for step in (lons - 2, lons - 1, 2, 3)]
    halo_to = [(lax.rem(pair + lons - 2 + 4 * x + i, lons), ch) for i in range(2)]

    def load_w(chip, who):
        columns = aligned((chip * 2 + who) * in_rows, 128, in_rows)
        return pltpu.make_async_copy(w_hbm.at[:, columns], wcol.at[pl.ds(0, 3 * taps)], load_sem.at[0])

    load_f = pltpu.make_async_copy(feat_hbm, raw.at[core], load_sem.at[1])
    loads = [
        pltpu.make_async_copy(cot_hbm.at[k], ext.at[pl.ds(BASES[k] + d + x * cols, cols)], load_sem.at[2 + k])
        for k, d in enumerate(DILATIONS)
    ]
    for copy in loads:
        copy.start()
    load_f.start()
    load_w(1 - xh, 1 - core).start()

    barrier = pltpu.get_barrier_semaphore()
    peers = [at(*hop) for hop in hops[0] + hops[1]] + [twin, mate, far] + outer
    for peer in peers:
        pl.semaphore_signal(barrier, inc=1, device_id=peer, device_id_type=MESH)
    pl.semaphore_wait(barrier, len(peers))

    def remote(src, dst, send, recv, peer):
        return pltpu.make_async_remote_copy(
            src_ref=src, dst_ref=dst, send_sem=send, recv_sem=recv, device_id=peer, device_id_type=MESH
        )

    inputs = []
    for k, d in enumerate(DILATIONS):
        base = BASES[k]
        mine = remote(
            cot_hbm.at[k], ext.at[pl.ds(base + d + x * cols, cols)], halo_send.at[3 * k], halo_recv.at[3 * k], twin
        )
        edges = [
            remote(
                cot_hbm.at[k, pl.ds(x * (cols - d), d)],
                ext.at[pl.ds(base + (1 - x) * (2 * cols + d), d)],
                halo_send.at[3 * k + 1 + i],
                halo_recv.at[3 * k + 1 + (1 - x)],
                halo_to[i],
            )
            for i in range(2)
        ]
        before = ext.at[pl.ds(base, d)]
        after = ext.at[pl.ds(base + 2 * cols + d, d)]
        arrivals = [
            remote(before, before, halo_send.at[3 * k + 1], halo_recv.at[3 * k + 1], halo_to[0]),
            remote(after, after, halo_send.at[3 * k + 1], halo_recv.at[3 * k + 2], halo_to[0]),
        ]
        inputs.append((mine, edges, arrivals))
    def send_branch(k):
        mine, edges, _ = inputs[k]
        for copy in edges + [mine]:
            copy.start()

    send_branch(0)
    feat_mate = remote(feat_hbm, raw.at[core], feat_send.at[0], feat_recv.at[0], mate)
    feat_far = remote(feat_hbm, raw.at[2 + core], feat_send.at[1], feat_recv.at[1], far)
    feat_on = remote(raw.at[2 + core], raw.at[2 + core], feat_send.at[2], feat_recv.at[2], mate)
    feat_mate.start()
    feat_far.start()

    lane = lax.broadcasted_iota(jnp.int32, (out_rows, 128), 1)

    def build(k, side, slot):
        d, base = DILATIONS[k], BASES[k]

        def column(m, carry):
            for lon_tap in range(3):
                v = ext[base + d + side * cols + m - d * (lon_tap - 1)].astype(jnp.float32)
                for lat_tap in range(3):
                    if lat_tap == 0:
                        moved = jnp.where(lane < 128 - d, pltpu.roll(v, 128 - d, 1), 0.0)
                    elif lat_tap == 1:
                        moved = v
                    else:
                        moved = jnp.where(lane >= d, pltpu.roll(v, d, 1), 0.0)
                    row = slot * taps + (lat_tap * 3 + lon_tap) * out_rows
                    stack[pl.ds(row, out_rows), aligned(m * 128, 128, 128)] = moved.astype(jnp.bfloat16)
            return carry

        lax.fori_loop(0, cols, column, 0)

    def flatten(chip):
        def column(m, carry):
            for jj in range(2):
                flat[pl.ds(jj * in_rows, in_rows), aligned(m * 128, 128, 128)] = raw[chip * 2 + jj, m]
            return carry

        lax.fori_loop(0, cols, column, 0)

    def order(e):
        far_side = (e >= 2) & (e < 5)
        return far_side, jnp.where(e < 2, e, jnp.where(far_side, e - 2, 2))

    def tile(h, block, sub, e):
        return part.at[e, aligned(mod4(here[h] + block) * rows, 8, rows), pl.ds(h * 256 + sub * 128, 128)]

    def rs1(e, h):
        up, down = at(*hops[h][0]), at(*hops[h][2])

        def send(i, src, peer):
            return remote(src, first.at[e, h, i], sum_send.at[e, h * 6 + i], sum_recv.at[e, h * 6 + i], peer)

        through = [send(0, tile(h, 2, 0, e), up), send(1, tile(h, 2, 1, e), down)]
        alone = [send(2, tile(h, 1, 1, e), up), send(3, tile(h, 3, 0, e), down)]
        both = [send(4, tile(h, 1, 0, e), up), send(5, tile(h, 3, 1, e), down)]
        return through, alone, both

    def piece(h, q, base_row=0, base_col=0):
        return (
            aligned(base_row + here[h] * rows + (q // 2) * (rows // 2), 8, rows // 2),
            aligned(base_col + h * 256 + lax.rem(q, 2) * 128, 128, 128),
        )

    def rs2(e, h):
        out = []
        for d in range(3):
            q = mod4(here[1 - h] + d + 1)
            slot = 12 + h * 3 + d
            r, c = piece(h, q)
            out.append(
                remote(part.at[e, r, c], second.at[e, h, d], sum_send.at[e, slot], sum_recv.at[e, slot], at(*hops[1 - h][d]))
            )
        return out

    def swap(e, h):
        return remote(low.at[e, h], third.at[e, h], sum_send.at[e, 18 + h], sum_recv.at[e, 18 + h], at(0, 0, 1))

    def corner(e):
        far_side, k = order(e)
        return k * taps, jnp.where(far_side, 1 - xh, xh) * 512

    def ag2_local(e, h):
        r, c = piece(h, here[1 - h], *corner(e))
        return pltpu.make_async_copy(low.at[e, h], kg_hbm.at[r, c], load_sem.at[5 + 2 * e + h])

    def ag2(e, h):
        r, c = piece(h, here[1 - h], *corner(e))
        return [
            remote(
                low.at[e, h], kg_hbm.at[r, c], sum_send.at[e, 20 + h * 3 + d], sum_recv.at[e, 20 + h * 3 + d], at(*hops[1 - h][d])
            )
            for d in range(3)
        ]

    def ag1(e, h):
        base_row, base_col = corner(e)
        up, down = at(*hops[h][0]), at(*hops[h][2])

        def send(i, block, sub, width, peer):
            area = kg_hbm.at[
                aligned(base_row + mod4(here[h] + block) * rows, 8, rows),
                aligned(base_col + h * 256 + sub * 128, 128, width),
            ]
            return remote(area, area, sum_send.at[e, 26 + h * 4 + i], sum_recv.at[e, 26 + h * 4 + i], peer)

        near = [send(0, 0, 0, 256, up), send(1, 0, 0, 256, down)]
        onward = [send(2, 3, 0, 128, up), send(3, 1, 1, 128, down)]
        return near, onward

    def do_chunk(e):
        far_side, k = order(e)
        slot = jnp.where(far_side, k, 3)
        for h in range(2):
            part[e, :, pl.ds(h * 256, 256)] = lax.dot_general(
                stack[aligned(slot * taps, 16, taps), :],
                flat[pl.ds(h * 256, 256), :],
                (((1,), (1,)), ((), ())),
                preferred_element_type=jnp.float32,
            )
            through, alone, _ = rs1(e, h)
            for copy in through + alone:
                copy.start()

    def do_rs1(e):
        for h in range(2):
            through, _, both = rs1(e, h)
            for i in range(2):
                through[i].wait()
                block, cols_at = (1, 3)[i], pl.ds(h * 256 + i * 128, 128)

                def step(n, carry):
                    r = aligned(mod4(here[h] + block) * rows + n * 16, 8, 16)
                    part[e, r, cols_at] = part[e, r, cols_at] + first[e, h, i, aligned(n * 16, 16, 16), :]
                    return carry

                lax.fori_loop(0, rows // 16, step, 0)
                both[i].start()

    def do_rs2(e):
        for h in range(2):
            _, alone, both = rs1(e, h)
            for copy in alone + both:
                copy.wait()

            def step(n, carry):
                r = aligned(n * 16, 16, 16)
                mine = aligned(here[h] * rows + n * 16, 8, 16)
                for sub, (a, b) in enumerate(((3, 4), (2, 5))):
                    c = pl.ds(h * 256 + sub * 128, 128)
                    part[e, mine, c] = part[e, mine, c] + (first[e, h, a, r, :] + first[e, h, b, r, :])
                return carry

            lax.fori_loop(0, rows // 16, step, 0)
            for copy in rs2(e, h):
                copy.start()

    def do_swap(e):
        for h in range(2):
            for copy in rs2(e, h):
                copy.wait()
            r, c = piece(h, here[1 - h])
            low[e, h] = (part[e, r, c] + second[e, h, 0]) + (second[e, h, 1] + second[e, h, 2])
            swap(e, h).start()

    def do_ag2(e):
        for h in range(2):
            swap(e, h).wait()
            low[e, h] = (low[e, h] + third[e, h]) * scale
            ag2_local(e, h).start()
            for copy in ag2(e, h):
                copy.start()

    def do_ag1(e):
        for h in range(2):
            ag2_local(e, h).wait()
            for copy in ag2(e, h):
                copy.wait()
            for copy in ag1(e, h)[0]:
                copy.start()

    def do_onward(e):
        for h in range(2):
            near, onward = ag1(e, h)
            near[1].wait_send()
            near[0].wait()
            onward[0].start()
            near[1].wait_recv()
            onward[1].start()

    def do_end(e):
        for h in range(2):
            for copy in ag1(e, h)[1]:
                copy.wait()

    wide = cols // GROUPS

    def turn(slot):
        wt[slot] = wcol[...].T

    def ig_group(slot, dst, q):
        def tile_of(i, carry):
            m = q * (wide // 2) + i
            res = jnp.dot(
                wt[slot], stack[pl.ds(0, wt.shape[2]), aligned(m * 256, 256, 256)], preferred_element_type=jnp.float32
            )
            prod[dst, 2 * m] = res[:, :128]
            prod[dst, 2 * m + 1] = res[:, 128:]
            return carry

        lax.fori_loop(0, wide // 2, tile_of, 0)

    def ig_mate(part_of, q):
        group = pl.ds(q * wide, wide)
        slot = part_of * GROUPS + q
        return remote(prod.at[0, group], other.at[part_of, group], ig_send.at[slot], ig_recv.at[slot], mate)

    def ig_far(q):
        group = pl.ds(q * wide, wide)
        slot = 2 * GROUPS + q
        return remote(prod.at[1, group], across.at[group], ig_send.at[slot], ig_recv.at[slot], far)

    def finish_far(q):
        ig_mate(1, q).wait()

        def column(i, carry):
            m = q * wide + i
            prod[1, m] = prod[1, m] + other[1, m]
            return carry

        lax.fori_loop(0, wide, column, 0)
        ig_far(q).start()

    def far_group(q):
        ig_group(0, 0, q)
        ig_mate(1, q).start()
        ig_group(1, 1, q)

        @pl.when(q > 0)
        def _():
            finish_far(q - 1)

    pad = wcol.shape[0] - 3 * taps
    wcol[pl.ds(3 * taps, pad), :] = jnp.zeros((pad, wcol.shape[1]), wcol.dtype)
    load_w(1 - xh, 1 - core).wait()
    turn(0)
    load_w(1 - xh, core).start()
    send_branch(1)
    load_w(1 - xh, core).wait()
    turn(1)
    load_w(xh, 1 - core).start()

    def arrived(k):
        mine, edges, arrivals = inputs[k]
        loads[k].wait()
        mine.wait_recv()
        for copy in arrivals:
            copy.wait_recv()

    def at_tick(u, work):
        early = (u == 0) | (u == 2)
        late = (u >= 4) & (u < 4 + CHUNKS - 2)

        @pl.when(early | late)
        def _():
            work(jnp.where(u < 4, lax.div(u, 2), u - 2))

    def body(s, carry):
        @pl.when(s == 0)
        def _():
            load_f.wait()
            feat_mate.wait()
            flatten(0)
            arrived(0)
            build(0, x, 3)

        @pl.when(s == 2)
        def _():
            arrived(1)
            build(1, x, 3)

        @pl.when(s == 4)
        def _():
            feat_far.wait()
            feat_on.start()
            build(0, 1 - x, 0)
            feat_on.wait()
            flatten(1)

        @pl.when(s == 5)
        def _():
            build(1, 1 - x, 1)

        @pl.when(s == 6)
        def _():
            arrived(2)
            build(2, 1 - x, 2)

        @pl.when(s == 7)
        def _():
            flatten(0)
            build(2, x, 3)

        at_tick(s, do_chunk)

        @pl.when(s == 0)
        def _():
            send_branch(2)

        @pl.when((s >= 7) & (s < 7 + GROUPS))
        def _():
            far_group(s - 7)

        @pl.when(s == 7 + GROUPS)
        def _():
            finish_far(GROUPS - 1)
            load_w(xh, 1 - core).wait()
            turn(0)
            load_w(xh, core).start()
            for k in range(3):
                build(k, x, k)
            load_w(xh, core).wait()
            turn(1)

        @pl.when((s >= 8 + GROUPS) & (s < 8 + 2 * GROUPS))
        def _():
            q = s - 8 - GROUPS
            ig_group(0, 0, q)
            ig_mate(0, q).start()
            ig_group(1, 2, q)

        for lag, work in zip(LAG[::-1], (do_onward, do_ag1, do_ag2, do_swap, do_rs2, do_rs1)):
            at_tick(s - lag, work)

        return carry

    lax.fori_loop(0, 8 + LAG[-1], body, 0)

    def last(q, carry):
        ig_mate(0, q).wait()
        ig_far(q).wait()

        def column(i, inner):
            m = q * wide + i
            ig[m] = (prod[2, m] + other[0, m] + across[m]).astype(jnp.bfloat16)
            return inner

        lax.fori_loop(0, wide, column, 0)
        return carry

    lax.fori_loop(0, GROUPS, last, 0)
    store = pltpu.make_async_copy(ig, ig_hbm, load_sem.at[0])
    store.start()
    for mine, edges, _ in inputs:
        mine.wait_send()
        for copy in edges:
            copy.wait_send()

    def end(e, carry):
        do_end(e)
        return carry

    lax.fori_loop(0, CHUNKS, end, 0)
    store.wait()


def local(features, cotangent, weights):
    in_rows, _, cols, lats = features.shape
    out_rows, in_total = weights.shape[3:]
    cells = cols * lats
    taps = 9 * out_rows
    rows = taps // 4
    depth = -(-3 * taps // 256) * 256
    scale = 1.0 / math.sqrt(cells * lax.axis_size("lon"))
    f32, bf16 = jnp.float32, jnp.bfloat16
    anywhere = pl.BlockSpec(memory_space=pl.ANY)
    ig, kg = pl.pallas_call(
        functools.partial(backward_kernel, scale),
        out_shape=(
            jax.ShapeDtypeStruct((cols, in_rows, lats), bf16),
            jax.ShapeDtypeStruct((3 * taps, in_total), f32),
        ),
        in_specs=[anywhere] * 3,
        out_specs=(anywhere, anywhere),
        scratch_shapes=[
            pltpu.VMEM((180, out_rows, lats), bf16),
            pltpu.VMEM((4 * taps, cells), bf16),
            pltpu.VMEM((4, cols, in_rows, lats), bf16),
            pltpu.VMEM((2 * in_rows, cells), bf16),
            pltpu.VMEM((depth, in_rows), bf16),
            pltpu.VMEM((2, in_rows, depth), bf16),
            pltpu.VMEM((CHUNKS, taps, 512), f32),
            pltpu.VMEM((CHUNKS, 2, 6, rows, 128), f32),
            pltpu.VMEM((CHUNKS, 2, 3, rows // 2, 128), f32),
            pltpu.VMEM((CHUNKS, 2, rows // 2, 128), f32),
            pltpu.VMEM((CHUNKS, 2, rows // 2, 128), f32),
            pltpu.VMEM((3, cols, in_rows, lats), f32),
            pltpu.VMEM((2, cols, in_rows, lats), f32),
            pltpu.VMEM((cols, in_rows, lats), f32),
            pltpu.VMEM((cols, in_rows, lats), bf16),
            pltpu.SemaphoreType.DMA((5 + 2 * CHUNKS,)),
            pltpu.SemaphoreType.DMA((9,)),
            pltpu.SemaphoreType.DMA((9,)),
            pltpu.SemaphoreType.DMA((3,)),
            pltpu.SemaphoreType.DMA((3,)),
            pltpu.SemaphoreType.DMA((CHUNKS, 34)),
            pltpu.SemaphoreType.DMA((CHUNKS, 34)),
            pltpu.SemaphoreType.DMA((3 * GROUPS,)),
            pltpu.SemaphoreType.DMA((3 * GROUPS,)),
        ],
        compiler_params=pltpu.CompilerParams(
            collective_id=1, has_side_effects=True, vmem_limit_bytes=52 * 1024 * 1024
        ),
        name="backward",
    )(
        features.reshape(in_rows, cols, lats).transpose(1, 0, 2),
        cotangent.reshape(3, out_rows, cols, lats).transpose(0, 2, 1, 3),
        weights.reshape(3 * taps, in_total),
    )
    input_grad = ig.transpose(1, 0, 2).reshape(in_rows, 1, cols, lats)
    return (input_grad, kg.reshape(3, 3, 3, out_rows, in_total))


def solution(mesh):
    return jax.shard_map(
        local,
        mesh=mesh,
        in_specs=(
            P("ch", None, "lon", None),
            P(None, "ch", None, "lon", None),
            P(None, None, None, "ch", None),
        ),
        out_specs=(P("ch", None, "lon", None), P(None, None, None, "ch", None)),
        check_vma=False,
    )
```

```python
import functools
import math

import jax
import jax.numpy as jnp
from jax import lax
from jax.experimental import pallas as pl
from jax.experimental.pallas import tpu as pltpu
from jax.sharding import PartitionSpec as P

DILATIONS = (6, 12, 18)
BASES = (0, 48, 108)
MESH = pl.DeviceIdType.MESH
Y, Z, X = 4, 4, 2
CHUNKS = 6
LAG = (1, 2, 3, 4, 5, 6)
GROUPS = 3


def mod4(v):
    return lax.rem(v, 4)


def aligned(v, m, size):
    return pl.ds(pl.multiple_of(v, m), size)


def backward_kernel(
    scale, feat_hbm, cot_hbm, w_hbm, ig_hbm, kg_hbm,
    ext, stack, raw, flat, wcol, wt, part, first, second, low, third, prod, other, across, ig,
    load_sem, halo_send, halo_recv, feat_send, feat_recv, sum_send, sum_recv, ig_send, ig_recv,
):
    lon = lax.axis_index("lon")
    ch = lax.axis_index("ch")
    lons = Y * Z * X
    y, z, x = lon // (Z * X), lax.rem(lon // X, Z), lax.rem(lon, X)
    xh, core = ch // 2, lax.rem(ch, 2)
    cols = feat_hbm.shape[0]
    in_rows = feat_hbm.shape[1]
    out_rows = cot_hbm.shape[2]
    taps = 9 * out_rows
    rows = taps // 4
    here = (y, z)

    def at(dy, dz, dx):
        return (mod4(y + dy) * (Z * X) + mod4(z + dz) * X + lax.rem(x + dx, X), ch)

    hops = [(d, 0, 0) for d in (1, 2, 3)], [(0, d, 0) for d in (1, 2, 3)]
    twin = at(0, 0, 1)
    pair = lon - x
    mate = (lon, xh * 2 + 1 - core)
    far = (pair + 1 - x, (1 - xh) * 2 + core)
    outer = [(lax.rem(pair + step, lons), ch) for step in (lons - 2, lons - 1, 2, 3)]
    halo_to = [(lax.rem(pair + lons - 2 + 4 * x + i, lons), ch) for i in range(2)]

    def load_w(chip, who):
        columns = aligned((chip * 2 + who) * in_rows, 128, in_rows)
        return pltpu.make_async_copy(w_hbm.at[:, columns], wcol.at[pl.ds(0, 3 * taps)], load_sem.at[0])

    load_f = pltpu.make_async_copy(feat_hbm, raw.at[core], load_sem.at[1])
    loads = [
        pltpu.make_async_copy(cot_hbm.at[k], ext.at[pl.ds(BASES[k] + d + x * cols, cols)], load_sem.at[2 + k])
        for k, d in enumerate(DILATIONS)
    ]
    for copy in loads:
        copy.start()
    load_f.start()
    load_w(1 - xh, 1 - core).start()

    barrier = pltpu.get_barrier_semaphore()
    peers = [at(*hop) for hop in hops[0] + hops[1]] + [twin, mate, far] + outer
    for peer in peers:
        pl.semaphore_signal(barrier, inc=1, device_id=peer, device_id_type=MESH)
    pl.semaphore_wait(barrier, len(peers))

    def remote(src, dst, send, recv, peer):
        return pltpu.make_async_remote_copy(
            src_ref=src, dst_ref=dst, send_sem=send, recv_sem=recv, device_id=peer, device_id_type=MESH
        )

    inputs = []
    for k, d in enumerate(DILATIONS):
        base = BASES[k]
        mine = remote(
            cot_hbm.at[k], ext.at[pl.ds(base + d + x * cols, cols)], halo_send.at[3 * k], halo_recv.at[3 * k], twin
        )
        edges = [
            remote(
                cot_hbm.at[k, pl.ds(x * (cols - d), d)],
                ext.at[pl.ds(base + (1 - x) * (2 * cols + d), d)],
                halo_send.at[3 * k + 1 + i],
                halo_recv.at[3 * k + 1 + (1 - x)],
                halo_to[i],
            )
            for i in range(2)
        ]
        for copy in edges + [mine]:
            copy.start()
        before = ext.at[pl.ds(base, d)]
        after = ext.at[pl.ds(base + 2 * cols + d, d)]
        arrivals = [
            remote(before, before, halo_send.at[3 * k + 1], halo_recv.at[3 * k + 1], halo_to[0]),
            remote(after, after, halo_send.at[3 * k + 1], halo_recv.at[3 * k + 2], halo_to[0]),
        ]
        inputs.append((mine, edges, arrivals))
    feat_mate = remote(feat_hbm, raw.at[core], feat_send.at[0], feat_recv.at[0], mate)
    feat_far = remote(feat_hbm, raw.at[2 + core], feat_send.at[1], feat_recv.at[1], far)
    feat_on = remote(raw.at[2 + core], raw.at[2 + core], feat_send.at[2], feat_recv.at[2], mate)
    feat_mate.start()
    feat_far.start()

    lane = lax.broadcasted_iota(jnp.int32, (out_rows, 128), 1)

    def build(k, side, slot):
        d, base = DILATIONS[k], BASES[k]

        def column(m, carry):
            for lon_tap in range(3):
                v = ext[base + d + side * cols + m - d * (lon_tap - 1)].astype(jnp.float32)
                for lat_tap in range(3):
                    if lat_tap == 0:
                        moved = jnp.where(lane < 128 - d, pltpu.roll(v, 128 - d, 1), 0.0)
                    elif lat_tap == 1:
                        moved = v
                    else:
                        moved = jnp.where(lane >= d, pltpu.roll(v, d, 1), 0.0)
                    row = slot * taps + (lat_tap * 3 + lon_tap) * out_rows
                    stack[pl.ds(row, out_rows), aligned(m * 128, 128, 128)] = moved.astype(jnp.bfloat16)
            return carry

        lax.fori_loop(0, cols, column, 0)

    def flatten(chip):
        def column(m, carry):
            for jj in range(2):
                flat[pl.ds(jj * in_rows, in_rows), aligned(m * 128, 128, 128)] = raw[chip * 2 + jj, m]
            return carry

        lax.fori_loop(0, cols, column, 0)

    def order(e):
        far_side = (e >= 2) & (e < 5)
        return far_side, jnp.where(e < 2, e, jnp.where(far_side, e - 2, 2))

    def tile(h, block, sub, e):
        return part.at[e, aligned(mod4(here[h] + block) * rows, 8, rows), pl.ds(h * 256 + sub * 128, 128)]

    def rs1(e, h):
        up, down = at(*hops[h][0]), at(*hops[h][2])

        def send(i, src, peer):
            return remote(src, first.at[e, h, i], sum_send.at[e, h * 6 + i], sum_recv.at[e, h * 6 + i], peer)

        through = [send(0, tile(h, 2, 0, e), up), send(1, tile(h, 2, 1, e), down)]
        alone = [send(2, tile(h, 1, 1, e), up), send(3, tile(h, 3, 0, e), down)]
        both = [send(4, tile(h, 1, 0, e), up), send(5, tile(h, 3, 1, e), down)]
        return through, alone, both

    def piece(h, q, base_row=0, base_col=0):
        return (
            aligned(base_row + here[h] * rows + (q // 2) * (rows // 2), 8, rows // 2),
            aligned(base_col + h * 256 + lax.rem(q, 2) * 128, 128, 128),
        )

    def rs2(e, h):
        out = []
        for d in range(3):
            q = mod4(here[1 - h] + d + 1)
            slot = 12 + h * 3 + d
            r, c = piece(h, q)
            out.append(
                remote(part.at[e, r, c], second.at[e, h, d], sum_send.at[e, slot], sum_recv.at[e, slot], at(*hops[1 - h][d]))
            )
        return out

    def swap(e, h):
        return remote(low.at[e, h], third.at[e, h], sum_send.at[e, 18 + h], sum_recv.at[e, 18 + h], at(0, 0, 1))

    def corner(e):
        far_side, k = order(e)
        return k * taps, jnp.where(far_side, 1 - xh, xh) * 512

    def ag2_local(e, h):
        r, c = piece(h, here[1 - h], *corner(e))
        return pltpu.make_async_copy(low.at[e, h], kg_hbm.at[r, c], load_sem.at[5 + 2 * e + h])

    def ag2(e, h):
        r, c = piece(h, here[1 - h], *corner(e))
        return [
            remote(
                low.at[e, h], kg_hbm.at[r, c], sum_send.at[e, 20 + h * 3 + d], sum_recv.at[e, 20 + h * 3 + d], at(*hops[1 - h][d])
            )
            for d in range(3)
        ]

    def ag1(e, h):
        base_row, base_col = corner(e)
        up, down = at(*hops[h][0]), at(*hops[h][2])

        def send(i, block, sub, width, peer):
            area = kg_hbm.at[
                aligned(base_row + mod4(here[h] + block) * rows, 8, rows),
                aligned(base_col + h * 256 + sub * 128, 128, width),
            ]
            return remote(area, area, sum_send.at[e, 26 + h * 4 + i], sum_recv.at[e, 26 + h * 4 + i], peer)

        near = [send(0, 0, 0, 256, up), send(1, 0, 0, 256, down)]
        onward = [send(2, 3, 0, 128, up), send(3, 1, 1, 128, down)]
        return near, onward

    def do_chunk(e):
        far_side, k = order(e)
        slot = jnp.where(far_side, k, 3)
        for h in range(2):
            part[e, :, pl.ds(h * 256, 256)] = lax.dot_general(
                stack[aligned(slot * taps, 16, taps), :],
                flat[pl.ds(h * 256, 256), :],
                (((1,), (1,)), ((), ())),
                preferred_element_type=jnp.float32,
            )
            through, alone, _ = rs1(e, h)
            for copy in through + alone:
                copy.start()

    def do_rs1(e):
        for h in range(2):
            through, _, both = rs1(e, h)
            for i in range(2):
                through[i].wait()
                block, cols_at = (1, 3)[i], pl.ds(h * 256 + i * 128, 128)

                def step(n, carry):
                    r = aligned(mod4(here[h] + block) * rows + n * 16, 8, 16)
                    part[e, r, cols_at] = part[e, r, cols_at] + first[e, h, i, aligned(n * 16, 16, 16), :]
                    return carry

                lax.fori_loop(0, rows // 16, step, 0)
                both[i].start()

    def do_rs2(e):
        for h in range(2):
            _, alone, both = rs1(e, h)
            for copy in alone + both:
                copy.wait()

            def step(n, carry):
                r = aligned(n * 16, 16, 16)
                mine = aligned(here[h] * rows + n * 16, 8, 16)
                for sub, (a, b) in enumerate(((3, 4), (2, 5))):
                    c = pl.ds(h * 256 + sub * 128, 128)
                    part[e, mine, c] = part[e, mine, c] + (first[e, h, a, r, :] + first[e, h, b, r, :])
                return carry

            lax.fori_loop(0, rows // 16, step, 0)
            for copy in rs2(e, h):
                copy.start()

    def do_swap(e):
        for h in range(2):
            for copy in rs2(e, h):
                copy.wait()
            r, c = piece(h, here[1 - h])
            low[e, h] = (part[e, r, c] + second[e, h, 0]) + (second[e, h, 1] + second[e, h, 2])
            swap(e, h).start()

    def do_ag2(e):
        for h in range(2):
            swap(e, h).wait()
            low[e, h] = (low[e, h] + third[e, h]) * scale
            ag2_local(e, h).start()
            for copy in ag2(e, h):
                copy.start()

    def do_ag1(e):
        for h in range(2):
            ag2_local(e, h).wait()
            for copy in ag2(e, h):
                copy.wait()
            for copy in ag1(e, h)[0]:
                copy.start()

    def do_onward(e):
        for h in range(2):
            near, onward = ag1(e, h)
            near[1].wait_send()
            near[0].wait()
            onward[0].start()
            near[1].wait_recv()
            onward[1].start()

    def do_end(e):
        for h in range(2):
            for copy in ag1(e, h)[1]:
                copy.wait()

    wide = cols // GROUPS

    def turn(slot):
        wt[slot] = wcol[...].T

    def ig_group(slot, dst, q):
        def tile_of(i, carry):
            m = q * (wide // 2) + i
            res = jnp.dot(
                wt[slot], stack[pl.ds(0, wt.shape[2]), aligned(m * 256, 256, 256)], preferred_element_type=jnp.float32
            )
            prod[dst, 2 * m] = res[:, :128]
            prod[dst, 2 * m + 1] = res[:, 128:]
            return carry

        lax.fori_loop(0, wide // 2, tile_of, 0)

    def ig_mate(part_of, q):
        group = pl.ds(q * wide, wide)
        slot = part_of * GROUPS + q
        return remote(prod.at[0, group], other.at[part_of, group], ig_send.at[slot], ig_recv.at[slot], mate)

    def ig_far(q):
        group = pl.ds(q * wide, wide)
        slot = 2 * GROUPS + q
        return remote(prod.at[1, group], across.at[group], ig_send.at[slot], ig_recv.at[slot], far)

    def finish_far(q):
        ig_mate(1, q).wait()

        def column(i, carry):
            m = q * wide + i
            prod[1, m] = prod[1, m] + other[1, m]
            return carry

        lax.fori_loop(0, wide, column, 0)
        ig_far(q).start()

    def far_group(q):
        ig_group(0, 0, q)
        ig_mate(1, q).start()
        ig_group(1, 1, q)

        @pl.when(q > 0)
        def _():
            finish_far(q - 1)

    pad = wcol.shape[0] - 3 * taps
    wcol[pl.ds(3 * taps, pad), :] = jnp.zeros((pad, wcol.shape[1]), wcol.dtype)
    load_w(1 - xh, 1 - core).wait()
    turn(0)
    load_w(1 - xh, core).start()
    load_w(1 - xh, core).wait()
    turn(1)
    load_w(xh, 1 - core).start()

    def arrived(k):
        mine, edges, arrivals = inputs[k]
        loads[k].wait()
        mine.wait_recv()
        for copy in arrivals:
            copy.wait_recv()

    def body(s, carry):
        @pl.when(s == 0)
        def _():
            load_f.wait()
            feat_mate.wait()
            flatten(0)
            arrived(0)
            build(0, x, 3)

        @pl.when(s == 1)
        def _():
            arrived(1)
            build(1, x, 3)

        @pl.when(s == 2)
        def _():
            feat_far.wait()
            feat_on.start()
            build(0, 1 - x, 0)
            feat_on.wait()
            flatten(1)

        @pl.when(s == 3)
        def _():
            build(1, 1 - x, 1)

        @pl.when(s == 4)
        def _():
            arrived(2)
            build(2, 1 - x, 2)

        @pl.when(s == 5)
        def _():
            flatten(0)
            build(2, x, 3)

        @pl.when(s < CHUNKS)
        def _():
            do_chunk(s)

        @pl.when((s >= 5) & (s < 5 + GROUPS))
        def _():
            far_group(s - 5)

        @pl.when(s == 5 + GROUPS)
        def _():
            finish_far(GROUPS - 1)

        @pl.when(s == 8)
        def _():
            load_w(xh, 1 - core).wait()
            turn(0)
            load_w(xh, core).start()
            for k in range(3):
                build(k, x, k)
            load_w(xh, core).wait()
            turn(1)

        @pl.when((s >= 9) & (s < 9 + GROUPS))
        def _():
            q = s - 9
            ig_group(0, 0, q)
            ig_mate(0, q).start()
            ig_group(1, 2, q)

        for lag, work in zip(LAG, (do_rs1, do_rs2, do_swap, do_ag2, do_ag1, do_onward)):

            @pl.when((s >= lag) & (s < CHUNKS + lag))
            def _():
                work(s - lag)

        return carry

    lax.fori_loop(0, CHUNKS + LAG[-1], body, 0)

    def last(q, carry):
        ig_mate(0, q).wait()
        ig_far(q).wait()

        def column(i, inner):
            m = q * wide + i
            ig[m] = (prod[2, m] + other[0, m] + across[m]).astype(jnp.bfloat16)
            return inner

        lax.fori_loop(0, wide, column, 0)
        return carry

    lax.fori_loop(0, GROUPS, last, 0)
    store = pltpu.make_async_copy(ig, ig_hbm, load_sem.at[0])
    store.start()
    for mine, edges, _ in inputs:
        mine.wait_send()
        for copy in edges:
            copy.wait_send()

    def end(e, carry):
        do_end(e)
        return carry

    lax.fori_loop(0, CHUNKS, end, 0)
    store.wait()


def local(features, cotangent, weights):
    in_rows, _, cols, lats = features.shape
    out_rows, in_total = weights.shape[3:]
    cells = cols * lats
    taps = 9 * out_rows
    rows = taps // 4
    depth = -(-3 * taps // 256) * 256
    scale = 1.0 / math.sqrt(cells * lax.axis_size("lon"))
    f32, bf16 = jnp.float32, jnp.bfloat16
    anywhere = pl.BlockSpec(memory_space=pl.ANY)
    ig, kg = pl.pallas_call(
        functools.partial(backward_kernel, scale),
        out_shape=(
            pltpu.VMEM((cols, in_rows, lats), bf16),
            pltpu.VMEM((3 * taps, in_total), f32),
        ),
        in_specs=[anywhere] * 3,
        out_specs=(anywhere, anywhere),
        scratch_shapes=[
            pltpu.VMEM((180, out_rows, lats), bf16),
            pltpu.VMEM((4 * taps, cells), bf16),
            pltpu.VMEM((4, cols, in_rows, lats), bf16),
            pltpu.VMEM((2 * in_rows, cells), bf16),
            pltpu.VMEM((depth, in_rows), bf16),
            pltpu.VMEM((2, in_rows, depth), bf16),
            pltpu.VMEM((CHUNKS, taps, 512), f32),
            pltpu.VMEM((CHUNKS, 2, 6, rows, 128), f32),
            pltpu.VMEM((CHUNKS, 2, 3, rows // 2, 128), f32),
            pltpu.VMEM((CHUNKS, 2, rows // 2, 128), f32),
            pltpu.VMEM((CHUNKS, 2, rows // 2, 128), f32),
            pltpu.VMEM((3, cols, in_rows, lats), f32),
            pltpu.VMEM((2, cols, in_rows, lats), f32),
            pltpu.VMEM((cols, in_rows, lats), f32),
            pltpu.VMEM((cols, in_rows, lats), bf16),
            pltpu.SemaphoreType.DMA((5 + 2 * CHUNKS,)),
            pltpu.SemaphoreType.DMA((9,)),
            pltpu.SemaphoreType.DMA((9,)),
            pltpu.SemaphoreType.DMA((3,)),
            pltpu.SemaphoreType.DMA((3,)),
            pltpu.SemaphoreType.DMA((CHUNKS, 34)),
            pltpu.SemaphoreType.DMA((CHUNKS, 34)),
            pltpu.SemaphoreType.DMA((3 * GROUPS,)),
            pltpu.SemaphoreType.DMA((3 * GROUPS,)),
        ],
        compiler_params=pltpu.CompilerParams(
            collective_id=1, has_side_effects=True, vmem_limit_bytes=52 * 1024 * 1024
        ),
        name="backward",
    )(
        features.reshape(in_rows, cols, lats).transpose(1, 0, 2),
        cotangent.reshape(3, out_rows, cols, lats).transpose(0, 2, 1, 3),
        weights.reshape(3 * taps, in_total),
    )
    input_grad = ig.transpose(1, 0, 2).reshape(in_rows, 1, cols, lats)
    return (input_grad, kg.reshape(3, 3, 3, out_rows, in_total))


def solution(mesh):
    return jax.shard_map(
        local,
        mesh=mesh,
        in_specs=(
            P("ch", None, "lon", None),
            P(None, "ch", None, "lon", None),
            P(None, None, None, "ch", None),
        ),
        out_specs=(P("ch", None, "lon", None), P(None, None, None, "ch", None)),
        check_vma=False,
    )
```

```python
import functools
import math

import jax
import jax.numpy as jnp
from jax import lax
from jax.experimental import pallas as pl
from jax.experimental.pallas import tpu as pltpu
from jax.sharding import PartitionSpec as P

DILATIONS = (6, 12, 18)
BASES = (0, 48, 108)
MESH = pl.DeviceIdType.MESH
Y, Z, X = 4, 4, 2
CHUNKS = 6
LAG = (1, 2, 3, 4, 5, 6)
GROUPS = 3


def mod4(v):
    return lax.rem(v, 4)


def aligned(v, m, size):
    return pl.ds(pl.multiple_of(v, m), size)


def backward_kernel(
    scale, feat_hbm, cot_hbm, w_hbm, ig_hbm, kg_hbm,
    ext, stack, raw, flat, wcol, wt, part, first, second, low, third, prod, other, across, ig,
    load_sem, halo_send, halo_recv, feat_send, feat_recv, sum_send, sum_recv, ig_send, ig_recv,
):
    lon = lax.axis_index("lon")
    ch = lax.axis_index("ch")
    lons = Y * Z * X
    y, z, x = lon // (Z * X), lax.rem(lon // X, Z), lax.rem(lon, X)
    xh, core = ch // 2, lax.rem(ch, 2)
    cols = feat_hbm.shape[0]
    in_rows = feat_hbm.shape[1]
    out_rows = cot_hbm.shape[2]
    taps = 9 * out_rows
    rows = taps // 4
    here = (y, z)

    def at(dy, dz, dx):
        return (mod4(y + dy) * (Z * X) + mod4(z + dz) * X + lax.rem(x + dx, X), ch)

    hops = [(d, 0, 0) for d in (1, 2, 3)], [(0, d, 0) for d in (1, 2, 3)]
    twin = at(0, 0, 1)
    pair = lon - x
    mate = (lon, xh * 2 + 1 - core)
    far = (pair + 1 - x, (1 - xh) * 2 + core)
    outer = [(lax.rem(pair + step, lons), ch) for step in (lons - 2, lons - 1, 2, 3)]
    halo_to = [(lax.rem(pair + lons - 2 + 4 * x + i, lons), ch) for i in range(2)]

    def load_w(chip, who):
        columns = aligned((chip * 2 + who) * in_rows, 128, in_rows)
        return pltpu.make_async_copy(w_hbm.at[:, columns], wcol.at[pl.ds(0, 3 * taps)], load_sem.at[0])

    load_f = pltpu.make_async_copy(feat_hbm, raw.at[core], load_sem.at[1])
    loads = [
        pltpu.make_async_copy(cot_hbm.at[k], ext.at[pl.ds(BASES[k] + d + x * cols, cols)], load_sem.at[2 + k])
        for k, d in enumerate(DILATIONS)
    ]
    for copy in loads:
        copy.start()
    load_f.start()
    load_w(1 - xh, 1 - core).start()

    barrier = pltpu.get_barrier_semaphore()
    peers = [at(*hop) for hop in hops[0] + hops[1]] + [twin, mate, far] + outer
    for peer in peers:
        pl.semaphore_signal(barrier, inc=1, device_id=peer, device_id_type=MESH)
    pl.semaphore_wait(barrier, len(peers))

    def remote(src, dst, send, recv, peer):
        return pltpu.make_async_remote_copy(
            src_ref=src, dst_ref=dst, send_sem=send, recv_sem=recv, device_id=peer, device_id_type=MESH
        )

    inputs = []
    for k, d in enumerate(DILATIONS):
        base = BASES[k]
        start = (1 - x) * (cols - d)
        mine = remote(
            cot_hbm.at[k, pl.ds(start, d)],
            ext.at[pl.ds(base + d + x * cols + start, d)],
            halo_send.at[3 * k],
            halo_recv.at[3 * k],
            twin,
        )
        edges = [
            remote(
                cot_hbm.at[k, pl.ds(x * (cols - d), d)],
                ext.at[pl.ds(base + (1 - x) * (2 * cols + d), d)],
                halo_send.at[3 * k + 1 + i],
                halo_recv.at[3 * k + 1 + (1 - x)],
                halo_to[i],
            )
            for i in range(2)
        ]
        for copy in edges + [mine]:
            copy.start()
        before = ext.at[pl.ds(base, d)]
        after = ext.at[pl.ds(base + 2 * cols + d, d)]
        arrivals = [
            remote(before, before, halo_send.at[3 * k + 1], halo_recv.at[3 * k + 1], halo_to[0]),
            remote(after, after, halo_send.at[3 * k + 1], halo_recv.at[3 * k + 2], halo_to[0]),
        ]
        inputs.append((mine, edges, arrivals))
    rests = []
    for k, d in enumerate(DILATIONS[:2]):
        rests.append(
            remote(
                cot_hbm.at[k, pl.ds(x * d, cols - d)],
                ext.at[pl.ds(BASES[k] + d + x * cols + x * d, cols - d)],
                halo_send.at[9 + k],
                halo_recv.at[9 + k],
                twin,
            )
        )
        rests[k].start()
    feat_mate = remote(feat_hbm, raw.at[core], feat_send.at[0], feat_recv.at[0], mate)
    feat_far = remote(feat_hbm, raw.at[2 + core], feat_send.at[1], feat_recv.at[1], far)
    feat_on = remote(raw.at[2 + core], raw.at[2 + core], feat_send.at[2], feat_recv.at[2], mate)
    feat_mate.start()
    feat_far.start()

    lane = lax.broadcasted_iota(jnp.int32, (out_rows, 128), 1)

    def build(k, side, slot):
        d, base = DILATIONS[k], BASES[k]

        def column(m, carry):
            for lon_tap in range(3):
                v = ext[base + d + side * cols + m - d * (lon_tap - 1)].astype(jnp.float32)
                for lat_tap in range(3):
                    if lat_tap == 0:
                        moved = jnp.where(lane < 128 - d, pltpu.roll(v, 128 - d, 1), 0.0)
                    elif lat_tap == 1:
                        moved = v
                    else:
                        moved = jnp.where(lane >= d, pltpu.roll(v, d, 1), 0.0)
                    row = slot * taps + (lat_tap * 3 + lon_tap) * out_rows
                    stack[pl.ds(row, out_rows), aligned(m * 128, 128, 128)] = moved.astype(jnp.bfloat16)
            return carry

        lax.fori_loop(0, cols, column, 0)

    def flatten(chip):
        def column(m, carry):
            for jj in range(2):
                flat[pl.ds(jj * in_rows, in_rows), aligned(m * 128, 128, 128)] = raw[chip * 2 + jj, m]
            return carry

        lax.fori_loop(0, cols, column, 0)

    def order(e):
        return e >= 3, lax.rem(e, 3)

    def tile(h, block, sub, e):
        return part.at[e, aligned(mod4(here[h] + block) * rows, 8, rows), pl.ds(h * 256 + sub * 128, 128)]

    def rs1(e, h):
        up, down = at(*hops[h][0]), at(*hops[h][2])

        def send(i, src, peer):
            return remote(src, first.at[e, h, i], sum_send.at[e, h * 6 + i], sum_recv.at[e, h * 6 + i], peer)

        through = [send(0, tile(h, 2, 0, e), up), send(1, tile(h, 2, 1, e), down)]
        alone = [send(2, tile(h, 1, 1, e), up), send(3, tile(h, 3, 0, e), down)]
        both = [send(4, tile(h, 1, 0, e), up), send(5, tile(h, 3, 1, e), down)]
        return through, alone, both

    def piece(h, q, base_row=0, base_col=0):
        return (
            aligned(base_row + here[h] * rows + (q // 2) * (rows // 2), 8, rows // 2),
            aligned(base_col + h * 256 + lax.rem(q, 2) * 128, 128, 128),
        )

    def rs2(e, h):
        out = []
        for d in range(3):
            q = mod4(here[1 - h] + d + 1)
            slot = 12 + h * 3 + d
            r, c = piece(h, q)
            out.append(
                remote(part.at[e, r, c], second.at[e, h, d], sum_send.at[e, slot], sum_recv.at[e, slot], at(*hops[1 - h][d]))
            )
        return out

    def swap(e, h):
        return remote(low.at[e, h], third.at[e, h], sum_send.at[e, 18 + h], sum_recv.at[e, 18 + h], at(0, 0, 1))

    def corner(e):
        far_side, k = order(e)
        return k * taps, jnp.where(far_side, 1 - xh, xh) * 512

    def ag2_local(e, h):
        r, c = piece(h, here[1 - h], *corner(e))
        return pltpu.make_async_copy(low.at[e, h], kg_hbm.at[r, c], load_sem.at[5 + 2 * e + h])

    def ag2(e, h):
        r, c = piece(h, here[1 - h], *corner(e))
        return [
            remote(
                low.at[e, h], kg_hbm.at[r, c], sum_send.at[e, 20 + h * 3 + d], sum_recv.at[e, 20 + h * 3 + d], at(*hops[1 - h][d])
            )
            for d in range(3)
        ]

    def ag1(e, h):
        base_row, base_col = corner(e)
        up, down = at(*hops[h][0]), at(*hops[h][2])

        def send(i, block, sub, width, peer):
            area = kg_hbm.at[
                aligned(base_row + mod4(here[h] + block) * rows, 8, rows),
                aligned(base_col + h * 256 + sub * 128, 128, width),
            ]
            return remote(area, area, sum_send.at[e, 26 + h * 4 + i], sum_recv.at[e, 26 + h * 4 + i], peer)

        near = [send(0, 0, 0, 256, up), send(1, 0, 0, 256, down)]
        onward = [send(2, 3, 0, 128, up), send(3, 1, 1, 128, down)]
        return near, onward

    def do_chunk(e):
        far_side, k = order(e)
        slot = jnp.where(far_side, k, 3)
        for h in range(2):
            part[e, :, pl.ds(h * 256, 256)] = lax.dot_general(
                stack[aligned(slot * taps, 16, taps), :],
                flat[pl.ds(h * 256, 256), :],
                (((1,), (1,)), ((), ())),
                preferred_element_type=jnp.float32,
            )
            through, alone, _ = rs1(e, h)
            for copy in through + alone:
                copy.start()

    def do_rs1(e):
        for h in range(2):
            through, _, both = rs1(e, h)
            for i in range(2):
                through[i].wait()
                block, cols_at = (1, 3)[i], pl.ds(h * 256 + i * 128, 128)

                def step(n, carry):
                    r = aligned(mod4(here[h] + block) * rows + n * 16, 8, 16)
                    part[e, r, cols_at] = part[e, r, cols_at] + first[e, h, i, aligned(n * 16, 16, 16), :]
                    return carry

                lax.fori_loop(0, rows // 16, step, 0)
                both[i].start()

    def do_rs2(e):
        for h in range(2):
            _, alone, both = rs1(e, h)
            for copy in alone + both:
                copy.wait()

            def step(n, carry):
                r = aligned(n * 16, 16, 16)
                mine = aligned(here[h] * rows + n * 16, 8, 16)
                for sub, (a, b) in enumerate(((3, 4), (2, 5))):
                    c = pl.ds(h * 256 + sub * 128, 128)
                    part[e, mine, c] = part[e, mine, c] + (first[e, h, a, r, :] + first[e, h, b, r, :])
                return carry

            lax.fori_loop(0, rows // 16, step, 0)
            for copy in rs2(e, h):
                copy.start()

    def do_swap(e):
        for h in range(2):
            for copy in rs2(e, h):
                copy.wait()
            r, c = piece(h, here[1 - h])
            low[e, h] = (part[e, r, c] + second[e, h, 0]) + (second[e, h, 1] + second[e, h, 2])
            swap(e, h).start()

    def do_ag2(e):
        for h in range(2):
            swap(e, h).wait()
            low[e, h] = (low[e, h] + third[e, h]) * scale
            ag2_local(e, h).start()
            for copy in ag2(e, h):
                copy.start()

    def do_ag1(e):
        for h in range(2):
            ag2_local(e, h).wait()
            for copy in ag2(e, h):
                copy.wait()
            for copy in ag1(e, h)[0]:
                copy.start()

    def do_onward(e):
        for h in range(2):
            near, onward = ag1(e, h)
            near[1].wait_send()
            near[0].wait()
            onward[0].start()
            near[1].wait_recv()
            onward[1].start()

    def do_end(e):
        for h in range(2):
            for copy in ag1(e, h)[1]:
                copy.wait()

    wide = cols // GROUPS

    def turn(slot):
        wt[slot] = wcol[...].T

    def ig_group(slot, dst, q):
        def tile_of(i, carry):
            m = q * (wide // 2) + i
            res = jnp.dot(
                wt[slot], stack[pl.ds(0, wt.shape[2]), aligned(m * 256, 256, 256)], preferred_element_type=jnp.float32
            )
            prod[dst, 2 * m] = res[:, :128]
            prod[dst, 2 * m + 1] = res[:, 128:]
            return carry

        lax.fori_loop(0, wide // 2, tile_of, 0)

    def ig_mate(part_of, q):
        group = pl.ds(q * wide, wide)
        slot = part_of * GROUPS + q
        return remote(prod.at[0, group], other.at[part_of, group], ig_send.at[slot], ig_recv.at[slot], mate)

    def ig_far(q):
        group = pl.ds(q * wide, wide)
        slot = 2 * GROUPS + q
        return remote(prod.at[1, group], across.at[group], ig_send.at[slot], ig_recv.at[slot], far)

    def finish_far(q):
        ig_mate(1, q).wait()

        def column(i, carry):
            m = q * wide + i
            prod[1, m] = prod[1, m] + other[1, m]
            return carry

        lax.fori_loop(0, wide, column, 0)
        ig_far(q).start()

    def far_group(q):
        ig_group(0, 0, q)
        ig_mate(1, q).start()
        ig_group(1, 1, q)

        @pl.when(q > 0)
        def _():
            finish_far(q - 1)

    pad = wcol.shape[0] - 3 * taps
    wcol[pl.ds(3 * taps, pad), :] = jnp.zeros((pad, wcol.shape[1]), wcol.dtype)
    load_w(1 - xh, 1 - core).wait()
    turn(0)
    load_w(1 - xh, core).start()
    load_w(1 - xh, core).wait()
    turn(1)
    load_w(xh, 1 - core).start()

    def arrived(k):
        mine, edges, arrivals = inputs[k]
        loads[k].wait()
        mine.wait_recv()
        for copy in arrivals:
            copy.wait_recv()

    def body(s, carry):
        @pl.when(s == 0)
        def _():
            load_f.wait()
            feat_mate.wait()
            flatten(0)
            arrived(0)
            build(0, x, 3)

        @pl.when(s == 1)
        def _():
            do_rs1(0)
            arrived(1)
            build(1, x, 3)

        @pl.when(s == 2)
        def _():
            arrived(2)
            build(2, x, 3)

        @pl.when(s == 3)
        def _():
            feat_far.wait()
            feat_on.start()
            rests[0].wait()
            build(0, 1 - x, 0)
            feat_on.wait()
            flatten(1)

        @pl.when(s == 4)
        def _():
            rests[1].wait()
            build(1, 1 - x, 1)

        @pl.when(s == 5)
        def _():
            build(2, 1 - x, 2)

        @pl.when(s < CHUNKS)
        def _():
            do_chunk(s)

        @pl.when((s >= 5) & (s < 5 + GROUPS))
        def _():
            far_group(s - 5)

        @pl.when(s == 5 + GROUPS)
        def _():
            finish_far(GROUPS - 1)

        @pl.when(s == 8)
        def _():
            load_w(xh, 1 - core).wait()
            turn(0)
            load_w(xh, core).start()
            for k in range(3):
                build(k, x, k)
            load_w(xh, core).wait()
            turn(1)

        @pl.when((s >= 9) & (s < 9 + GROUPS))
        def _():
            q = s - 9
            ig_group(0, 0, q)
            ig_mate(0, q).start()
            ig_group(1, 2, q)

        for lag, work in zip(LAG, (do_rs1, do_rs2, do_swap, do_ag2, do_ag1, do_onward)):
            ahead = (s == lag - 1) if lag > 1 else False

            @pl.when(ahead | ((s > lag) & (s < CHUNKS + lag)))
            def _():
                work(jnp.where(s < lag, 0, s - lag))

        return carry

    lax.fori_loop(0, CHUNKS + LAG[-1], body, 0)

    def last(q, carry):
        ig_mate(0, q).wait()
        ig_far(q).wait()

        def column(i, inner):
            m = q * wide + i
            ig[m] = (prod[2, m] + other[0, m] + across[m]).astype(jnp.bfloat16)
            return inner

        lax.fori_loop(0, wide, column, 0)
        return carry

    lax.fori_loop(0, GROUPS, last, 0)
    store = pltpu.make_async_copy(ig, ig_hbm, load_sem.at[0])
    store.start()
    for mine, edges, _ in inputs:
        mine.wait_send()
        for copy in edges:
            copy.wait_send()

    def end(e, carry):
        do_end(e)
        return carry

    lax.fori_loop(0, CHUNKS, end, 0)
    store.wait()


def local(features, cotangent, weights):
    in_rows, _, cols, lats = features.shape
    out_rows, in_total = weights.shape[3:]
    cells = cols * lats
    taps = 9 * out_rows
    rows = taps // 4
    depth = -(-3 * taps // 256) * 256
    scale = 1.0 / math.sqrt(cells * lax.axis_size("lon"))
    f32, bf16 = jnp.float32, jnp.bfloat16
    anywhere = pl.BlockSpec(memory_space=pl.ANY)
    ig, kg = pl.pallas_call(
        functools.partial(backward_kernel, scale),
        out_shape=(
            pltpu.VMEM((cols, in_rows, lats), bf16),
            pltpu.VMEM((3 * taps, in_total), f32),
        ),
        in_specs=[anywhere] * 3,
        out_specs=(anywhere, anywhere),
        scratch_shapes=[
            pltpu.VMEM((180, out_rows, lats), bf16),
            pltpu.VMEM((4 * taps, cells), bf16),
            pltpu.VMEM((4, cols, in_rows, lats), bf16),
            pltpu.VMEM((2 * in_rows, cells), bf16),
            pltpu.VMEM((depth, in_rows), bf16),
            pltpu.VMEM((2, in_rows, depth), bf16),
            pltpu.VMEM((CHUNKS, taps, 512), f32),
            pltpu.VMEM((CHUNKS, 2, 6, rows, 128), f32),
            pltpu.VMEM((CHUNKS, 2, 3, rows // 2, 128), f32),
            pltpu.VMEM((CHUNKS, 2, rows // 2, 128), f32),
            pltpu.VMEM((CHUNKS, 2, rows // 2, 128), f32),
            pltpu.VMEM((3, cols, in_rows, lats), f32),
            pltpu.VMEM((2, cols, in_rows, lats), f32),
            pltpu.VMEM((cols, in_rows, lats), f32),
            pltpu.VMEM((cols, in_rows, lats), bf16),
            pltpu.SemaphoreType.DMA((5 + 2 * CHUNKS,)),
            pltpu.SemaphoreType.DMA((11,)),
            pltpu.SemaphoreType.DMA((11,)),
            pltpu.SemaphoreType.DMA((3,)),
            pltpu.SemaphoreType.DMA((3,)),
            pltpu.SemaphoreType.DMA((CHUNKS, 34)),
            pltpu.SemaphoreType.DMA((CHUNKS, 34)),
            pltpu.SemaphoreType.DMA((3 * GROUPS,)),
            pltpu.SemaphoreType.DMA((3 * GROUPS,)),
        ],
        compiler_params=pltpu.CompilerParams(
            collective_id=1, has_side_effects=True, vmem_limit_bytes=52 * 1024 * 1024
        ),
        name="backward",
    )(
        features.reshape(in_rows, cols, lats).transpose(1, 0, 2),
        cotangent.reshape(3, out_rows, cols, lats).transpose(0, 2, 1, 3),
        weights.reshape(3 * taps, in_total),
    )
    input_grad = ig.transpose(1, 0, 2).reshape(in_rows, 1, cols, lats)
    return (input_grad, kg.reshape(3, 3, 3, out_rows, in_total))


def solution(mesh):
    return jax.shard_map(
        local,
        mesh=mesh,
        in_specs=(
            P("ch", None, "lon", None),
            P(None, "ch", None, "lon", None),
            P(None, None, None, "ch", None),
        ),
        out_specs=(P("ch", None, "lon", None), P(None, None, None, "ch", None)),
        check_vma=False,
    )
```

```python
import functools
import math

import jax
import jax.numpy as jnp
from jax import lax
from jax.experimental import pallas as pl
from jax.experimental.pallas import tpu as pltpu
from jax.sharding import PartitionSpec as P

DILATIONS = (6, 12, 18)
BASES = (0, 48, 108)
MESH = pl.DeviceIdType.MESH
Y, Z, X = 4, 4, 2
CHUNKS = 6
LAG = (1, 2, 3, 4, 5, 6)
GROUPS = 3


def mod4(v):
    return lax.rem(v, 4)


def aligned(v, m, size):
    return pl.ds(pl.multiple_of(v, m), size)


def backward_kernel(
    scale, feat_hbm, cot_hbm, w_hbm, ig_hbm, kg_hbm,
    ext, stack, raw, flat, wcol, wt, part, first, second, low, third, prod, other, across, ig,
    load_sem, halo_send, halo_recv, feat_send, feat_recv, sum_send, sum_recv, ig_send, ig_recv,
):
    lon = lax.axis_index("lon")
    ch = lax.axis_index("ch")
    lons = Y * Z * X
    y, z, x = lon // (Z * X), lax.rem(lon // X, Z), lax.rem(lon, X)
    xh, core = ch // 2, lax.rem(ch, 2)
    cols = feat_hbm.shape[0]
    in_rows = feat_hbm.shape[1]
    out_rows = cot_hbm.shape[2]
    taps = 9 * out_rows
    rows = taps // 4
    here = (y, z)

    def at(dy, dz, dx):
        return (mod4(y + dy) * (Z * X) + mod4(z + dz) * X + lax.rem(x + dx, X), ch)

    hops = [(d, 0, 0) for d in (1, 2, 3)], [(0, d, 0) for d in (1, 2, 3)]
    twin = at(0, 0, 1)
    pair = lon - x
    mate = (lon, xh * 2 + 1 - core)
    far = (pair + 1 - x, (1 - xh) * 2 + core)
    outer = [(lax.rem(pair + step, lons), ch) for step in (lons - 2, lons - 1, 2, 3)]
    halo_to = [(lax.rem(pair + lons - 2 + 4 * x + i, lons), ch) for i in range(2)]

    def load_w(chip, who):
        columns = aligned((chip * 2 + who) * in_rows, 128, in_rows)
        return pltpu.make_async_copy(w_hbm.at[:, columns], wcol.at[pl.ds(0, 3 * taps)], load_sem.at[0])

    load_f = pltpu.make_async_copy(feat_hbm, raw.at[core], load_sem.at[1])
    loads = [
        pltpu.make_async_copy(cot_hbm.at[k], ext.at[pl.ds(BASES[k] + d + x * cols, cols)], load_sem.at[2 + k])
        for k, d in enumerate(DILATIONS)
    ]
    for copy in loads:
        copy.start()
    load_f.start()
    load_w(1 - xh, 1 - core).start()

    barrier = pltpu.get_barrier_semaphore()
    peers = [at(*hop) for hop in hops[0] + hops[1]] + [twin, mate, far] + outer
    for peer in peers:
        pl.semaphore_signal(barrier, inc=1, device_id=peer, device_id_type=MESH)
    pl.semaphore_wait(barrier, len(peers))

    def remote(src, dst, send, recv, peer):
        return pltpu.make_async_remote_copy(
            src_ref=src, dst_ref=dst, send_sem=send, recv_sem=recv, device_id=peer, device_id_type=MESH
        )

    inputs = []
    for k, d in enumerate(DILATIONS):
        base = BASES[k]
        start = (1 - x) * (cols - d)
        mine = remote(
            cot_hbm.at[k, pl.ds(start, d)],
            ext.at[pl.ds(base + d + x * cols + start, d)],
            halo_send.at[3 * k],
            halo_recv.at[3 * k],
            twin,
        )
        edges = [
            remote(
                cot_hbm.at[k, pl.ds(x * (cols - d), d)],
                ext.at[pl.ds(base + (1 - x) * (2 * cols + d), d)],
                halo_send.at[3 * k + 1 + i],
                halo_recv.at[3 * k + 1 + (1 - x)],
                halo_to[i],
            )
            for i in range(2)
        ]
        for copy in edges + [mine]:
            copy.start()
        before = ext.at[pl.ds(base, d)]
        after = ext.at[pl.ds(base + 2 * cols + d, d)]
        arrivals = [
            remote(before, before, halo_send.at[3 * k + 1], halo_recv.at[3 * k + 1], halo_to[0]),
            remote(after, after, halo_send.at[3 * k + 1], halo_recv.at[3 * k + 2], halo_to[0]),
        ]
        inputs.append((mine, edges, arrivals))
    rests = []
    for k, d in enumerate(DILATIONS[:2]):
        rests.append(
            remote(
                cot_hbm.at[k, pl.ds(x * d, cols - d)],
                ext.at[pl.ds(BASES[k] + d + x * cols + x * d, cols - d)],
                halo_send.at[9 + k],
                halo_recv.at[9 + k],
                twin,
            )
        )
        rests[k].start()
    feat_mate = remote(feat_hbm, raw.at[core], feat_send.at[0], feat_recv.at[0], mate)
    feat_far = remote(feat_hbm, raw.at[2 + core], feat_send.at[1], feat_recv.at[1], far)
    feat_on = remote(raw.at[2 + core], raw.at[2 + core], feat_send.at[2], feat_recv.at[2], mate)
    feat_mate.start()
    feat_far.start()

    lane = lax.broadcasted_iota(jnp.int32, (out_rows, 128), 1)

    def build(k, side, slot):
        d, base = DILATIONS[k], BASES[k]

        def column(m, carry):
            for lon_tap in range(3):
                v = ext[base + d + side * cols + m - d * (lon_tap - 1)]
                for lat_tap in range(3):
                    if lat_tap == 0:
                        moved = pltpu.roll(v, 128 - d, 1) * (lane < 128 - d).astype(v.dtype)
                    elif lat_tap == 1:
                        moved = v
                    else:
                        moved = pltpu.roll(v, d, 1) * (lane >= d).astype(v.dtype)
                    row = slot * taps + (lat_tap * 3 + lon_tap) * out_rows
                    stack[pl.ds(row, out_rows), aligned(m * 128, 128, 128)] = moved
            return carry

        lax.fori_loop(0, cols, column, 0)

    def flatten(chip):
        def column(m, carry):
            for jj in range(2):
                flat[pl.ds(jj * in_rows, in_rows), aligned(m * 128, 128, 128)] = raw[chip * 2 + jj, m]
            return carry

        lax.fori_loop(0, cols, column, 0)

    def order(e):
        return e >= 3, lax.rem(e, 3)

    def tile(h, block, sub, e):
        return part.at[e, aligned(mod4(here[h] + block) * rows, 8, rows), pl.ds(h * 256 + sub * 128, 128)]

    def rs1(e, h):
        up, down = at(*hops[h][0]), at(*hops[h][2])

        def send(i, src, peer):
            return remote(src, first.at[e, h, i], sum_send.at[e, h * 6 + i], sum_recv.at[e, h * 6 + i], peer)

        through = [send(0, tile(h, 2, 0, e), up), send(1, tile(h, 2, 1, e), down)]
        alone = [send(2, tile(h, 1, 1, e), up), send(3, tile(h, 3, 0, e), down)]
        both = [send(4, tile(h, 1, 0, e), up), send(5, tile(h, 3, 1, e), down)]
        return through, alone, both

    def piece(h, q, base_row=0, base_col=0):
        return (
            aligned(base_row + here[h] * rows + (q // 2) * (rows // 2), 8, rows // 2),
            aligned(base_col + h * 256 + lax.rem(q, 2) * 128, 128, 128),
        )

    def rs2(e, h):
        out = []
        for d in range(3):
            q = mod4(here[1 - h] + d + 1)
            slot = 12 + h * 3 + d
            r, c = piece(h, q)
            out.append(
                remote(part.at[e, r, c], second.at[e, h, d], sum_send.at[e, slot], sum_recv.at[e, slot], at(*hops[1 - h][d]))
            )
        return out

    def swap(e, h):
        return remote(low.at[e, h], third.at[e, h], sum_send.at[e, 18 + h], sum_recv.at[e, 18 + h], at(0, 0, 1))

    def corner(e):
        far_side, k = order(e)
        return k * taps, jnp.where(far_side, 1 - xh, xh) * 512

    def ag2_local(e, h):
        r, c = piece(h, here[1 - h], *corner(e))
        return pltpu.make_async_copy(low.at[e, h], kg_hbm.at[r, c], load_sem.at[5 + 2 * e + h])

    def ag2(e, h):
        r, c = piece(h, here[1 - h], *corner(e))
        return [
            remote(
                low.at[e, h], kg_hbm.at[r, c], sum_send.at[e, 20 + h * 3 + d], sum_recv.at[e, 20 + h * 3 + d], at(*hops[1 - h][d])
            )
            for d in range(3)
        ]

    def ag1(e, h):
        base_row, base_col = corner(e)
        up, down = at(*hops[h][0]), at(*hops[h][2])

        def send(i, block, sub, width, peer):
            area = kg_hbm.at[
                aligned(base_row + mod4(here[h] + block) * rows, 8, rows),
                aligned(base_col + h * 256 + sub * 128, 128, width),
            ]
            return remote(area, area, sum_send.at[e, 26 + h * 4 + i], sum_recv.at[e, 26 + h * 4 + i], peer)

        near = [send(0, 0, 0, 256, up), send(1, 0, 0, 256, down)]
        onward = [send(2, 3, 0, 128, up), send(3, 1, 1, 128, down)]
        return near, onward

    def do_chunk(e):
        far_side, k = order(e)
        slot = jnp.where(far_side, k, 3)
        for h in range(2):
            part[e, :, pl.ds(h * 256, 256)] = lax.dot_general(
                stack[aligned(slot * taps, 16, taps), :],
                flat[pl.ds(h * 256, 256), :],
                (((1,), (1,)), ((), ())),
                preferred_element_type=jnp.float32,
            )
            through, alone, _ = rs1(e, h)
            for copy in through + alone:
                copy.start()

    def do_rs1(e):
        for h in range(2):
            through, _, both = rs1(e, h)
            for i in range(2):
                through[i].wait()
                block, cols_at = (1, 3)[i], pl.ds(h * 256 + i * 128, 128)

                def step(n, carry):
                    r = aligned(mod4(here[h] + block) * rows + n * 16, 8, 16)
                    part[e, r, cols_at] = part[e, r, cols_at] + first[e, h, i, aligned(n * 16, 16, 16), :]
                    return carry

                lax.fori_loop(0, rows // 16, step, 0)
                both[i].start()

    def do_rs2(e):
        for h in range(2):
            _, alone, both = rs1(e, h)
            for copy in alone + both:
                copy.wait()

            def step(n, carry):
                r = aligned(n * 16, 16, 16)
                mine = aligned(here[h] * rows + n * 16, 8, 16)
                for sub, (a, b) in enumerate(((3, 4), (2, 5))):
                    c = pl.ds(h * 256 + sub * 128, 128)
                    part[e, mine, c] = part[e, mine, c] + (first[e, h, a, r, :] + first[e, h, b, r, :])
                return carry

            lax.fori_loop(0, rows // 16, step, 0)
            for copy in rs2(e, h):
                copy.start()

    def do_swap(e):
        for h in range(2):
            for copy in rs2(e, h):
                copy.wait()
            r, c = piece(h, here[1 - h])
            low[e, h] = (part[e, r, c] + second[e, h, 0]) + (second[e, h, 1] + second[e, h, 2])
            swap(e, h).start()

    def do_ag2(e):
        for h in range(2):
            swap(e, h).wait()
            low[e, h] = (low[e, h] + third[e, h]) * scale
            ag2_local(e, h).start()
            for copy in ag2(e, h):
                copy.start()

    def do_ag1(e):
        for h in range(2):
            ag2_local(e, h).wait()
            for copy in ag2(e, h):
                copy.wait()
            for copy in ag1(e, h)[0]:
                copy.start()

    def do_onward(e):
        for h in range(2):
            near, onward = ag1(e, h)
            near[1].wait_send()
            near[0].wait()
            onward[0].start()
            near[1].wait_recv()
            onward[1].start()

    def do_end(e):
        for h in range(2):
            for copy in ag1(e, h)[1]:
                copy.wait()

    wide = cols // GROUPS

    def turn(slot):
        wt[slot] = wcol[...].T

    def ig_group(slot, dst, q):
        def tile_of(i, carry):
            m = q * (wide // 2) + i
            res = jnp.dot(
                wt[slot], stack[pl.ds(0, wt.shape[2]), aligned(m * 256, 256, 256)], preferred_element_type=jnp.float32
            )
            prod[dst, 2 * m] = res[:, :128]
            prod[dst, 2 * m + 1] = res[:, 128:]
            return carry

        lax.fori_loop(0, wide // 2, tile_of, 0)

    def ig_mate(part_of, q):
        group = pl.ds(q * wide, wide)
        slot = part_of * GROUPS + q
        return remote(prod.at[0, group], other.at[part_of, group], ig_send.at[slot], ig_recv.at[slot], mate)

    def ig_far(q):
        group = pl.ds(q * wide, wide)
        slot = 2 * GROUPS + q
        return remote(prod.at[1, group], across.at[group], ig_send.at[slot], ig_recv.at[slot], far)

    def finish_far(q):
        ig_mate(1, q).wait()

        def column(i, carry):
            m = q * wide + i
            prod[1, m] = prod[1, m] + other[1, m]
            return carry

        lax.fori_loop(0, wide, column, 0)
        ig_far(q).start()

    def far_group(q):
        ig_group(0, 0, q)
        ig_mate(1, q).start()
        ig_group(1, 1, q)

        @pl.when(q > 0)
        def _():
            finish_far(q - 1)

    pad = wcol.shape[0] - 3 * taps
    wcol[pl.ds(3 * taps, pad), :] = jnp.zeros((pad, wcol.shape[1]), wcol.dtype)
    load_w(1 - xh, 1 - core).wait()
    turn(0)
    load_w(1 - xh, core).start()
    load_w(1 - xh, core).wait()
    turn(1)
    load_w(xh, 1 - core).start()

    def arrived(k):
        mine, edges, arrivals = inputs[k]
        loads[k].wait()
        mine.wait_recv()
        for copy in arrivals:
            copy.wait_recv()

    def body(s, carry):
        @pl.when(s == 0)
        def _():
            load_f.wait()
            feat_mate.wait()
            flatten(0)
            arrived(0)
            build(0, x, 3)

        @pl.when(s == 1)
        def _():
            do_rs1(0)
            arrived(1)
            build(1, x, 3)

        @pl.when(s == 2)
        def _():
            arrived(2)
            build(2, x, 3)

        @pl.when(s == 3)
        def _():
            feat_far.wait()
            feat_on.start()
            for k in range(3):
                if k < 2:
                    rests[k].wait()
                build(k, 1 - x, k)
            feat_on.wait()
            flatten(1)

        @pl.when(s < CHUNKS)
        def _():
            do_chunk(s)

        @pl.when((s >= 3) & (s < 3 + GROUPS))
        def _():
            far_group(s - 3)

        @pl.when(s == 3 + GROUPS)
        def _():
            finish_far(GROUPS - 1)

        @pl.when(s == 7)
        def _():
            load_w(xh, 1 - core).wait()
            turn(0)
            load_w(xh, core).start()
            for k in range(3):
                build(k, x, k)
            load_w(xh, core).wait()
            turn(1)

        @pl.when((s >= 8) & (s < 8 + GROUPS))
        def _():
            q = s - 8
            ig_group(0, 0, q)
            ig_mate(0, q).start()
            ig_group(1, 2, q)

        for lag, work in zip(LAG, (do_rs1, do_rs2, do_swap, do_ag2, do_ag1, do_onward)):
            ahead = (s == lag - 1) if lag > 1 else False

            @pl.when(ahead | ((s > lag) & (s < CHUNKS + lag)))
            def _():
                work(jnp.where(s < lag, 0, s - lag))

        return carry

    lax.fori_loop(0, CHUNKS + LAG[-1], body, 0)

    def last(q, carry):
        ig_mate(0, q).wait()
        ig_far(q).wait()

        def column(i, inner):
            m = q * wide + i
            ig[m] = (prod[2, m] + other[0, m] + across[m]).astype(jnp.bfloat16)
            return inner

        lax.fori_loop(0, wide, column, 0)
        return carry

    lax.fori_loop(0, GROUPS, last, 0)
    store = pltpu.make_async_copy(ig, ig_hbm, load_sem.at[0])
    store.start()
    for mine, edges, _ in inputs:
        mine.wait_send()
        for copy in edges:
            copy.wait_send()

    def end(e, carry):
        do_end(e)
        return carry

    lax.fori_loop(0, CHUNKS, end, 0)
    store.wait()


def local(features, cotangent, weights):
    in_rows, _, cols, lats = features.shape
    out_rows, in_total = weights.shape[3:]
    cells = cols * lats
    taps = 9 * out_rows
    rows = taps // 4
    depth = -(-3 * taps // 256) * 256
    scale = 1.0 / math.sqrt(cells * lax.axis_size("lon"))
    f32, bf16 = jnp.float32, jnp.bfloat16
    anywhere = pl.BlockSpec(memory_space=pl.ANY)
    ig, kg = pl.pallas_call(
        functools.partial(backward_kernel, scale),
        out_shape=(
            pltpu.VMEM((cols, in_rows, lats), bf16),
            pltpu.VMEM((3 * taps, in_total), f32),
        ),
        in_specs=[anywhere] * 3,
        out_specs=(anywhere, anywhere),
        scratch_shapes=[
            pltpu.VMEM((180, out_rows, lats), bf16),
            pltpu.VMEM((4 * taps, cells), bf16),
            pltpu.VMEM((4, cols, in_rows, lats), bf16),
            pltpu.VMEM((2 * in_rows, cells), bf16),
            pltpu.VMEM((depth, in_rows), bf16),
            pltpu.VMEM((2, in_rows, depth), bf16),
            pltpu.VMEM((CHUNKS, taps, 512), f32),
            pltpu.VMEM((CHUNKS, 2, 6, rows, 128), f32),
            pltpu.VMEM((CHUNKS, 2, 3, rows // 2, 128), f32),
            pltpu.VMEM((CHUNKS, 2, rows // 2, 128), f32),
            pltpu.VMEM((CHUNKS, 2, rows // 2, 128), f32),
            pltpu.VMEM((3, cols, in_rows, lats), f32),
            pltpu.VMEM((2, cols, in_rows, lats), f32),
            pltpu.VMEM((cols, in_rows, lats), f32),
            pltpu.VMEM((cols, in_rows, lats), bf16),
            pltpu.SemaphoreType.DMA((5 + 2 * CHUNKS,)),
            pltpu.SemaphoreType.DMA((11,)),
            pltpu.SemaphoreType.DMA((11,)),
            pltpu.SemaphoreType.DMA((3,)),
            pltpu.SemaphoreType.DMA((3,)),
            pltpu.SemaphoreType.DMA((CHUNKS, 34)),
            pltpu.SemaphoreType.DMA((CHUNKS, 34)),
            pltpu.SemaphoreType.DMA((3 * GROUPS,)),
            pltpu.SemaphoreType.DMA((3 * GROUPS,)),
        ],
        compiler_params=pltpu.CompilerParams(
            collective_id=1, has_side_effects=True, vmem_limit_bytes=52 * 1024 * 1024
        ),
        name="backward",
    )(
        features.reshape(in_rows, cols, lats).transpose(1, 0, 2),
        cotangent.reshape(3, out_rows, cols, lats).transpose(0, 2, 1, 3),
        weights.reshape(3 * taps, in_total),
    )
    input_grad = ig.transpose(1, 0, 2).reshape(in_rows, 1, cols, lats)
    return (input_grad, kg.reshape(3, 3, 3, out_rows, in_total))


def solution(mesh):
    return jax.shard_map(
        local,
        mesh=mesh,
        in_specs=(
            P("ch", None, "lon", None),
            P(None, "ch", None, "lon", None),
            P(None, None, None, "ch", None),
        ),
        out_specs=(P("ch", None, "lon", None), P(None, None, None, "ch", None)),
        check_vma=False,
    )
```

```python
import functools
import math

import jax
import jax.numpy as jnp
from jax import lax
from jax.experimental import pallas as pl
from jax.experimental.pallas import tpu as pltpu
from jax.sharding import PartitionSpec as P

DILATIONS = (6, 12, 18)
BASES = (0, 48, 108)
MESH = pl.DeviceIdType.MESH
Y, Z, X = 4, 4, 2
CHUNKS = 6
LAG = (1, 2, 3, 4, 5, 6)
GROUPS = 3


def mod4(v):
    return lax.rem(v, 4)


def aligned(v, m, size):
    return pl.ds(pl.multiple_of(v, m), size)


def backward_kernel(
    scale, feat_hbm, cot_hbm, w_hbm, ig_hbm, kg_hbm,
    ext, stack, raw, flat, wcol, wt, part, first, second, low, third, prod, other, across, ig,
    load_sem, halo_send, halo_recv, feat_send, feat_recv, sum_send, sum_recv, ig_send, ig_recv,
):
    lon = lax.axis_index("lon")
    ch = lax.axis_index("ch")
    lons = Y * Z * X
    y, z, x = lon // (Z * X), lax.rem(lon // X, Z), lax.rem(lon, X)
    xh, core = ch // 2, lax.rem(ch, 2)
    cols = feat_hbm.shape[0]
    in_rows = feat_hbm.shape[1]
    out_rows = cot_hbm.shape[2]
    taps = 9 * out_rows
    rows = taps // 4
    here = (y, z)

    def at(dy, dz, dx):
        return (mod4(y + dy) * (Z * X) + mod4(z + dz) * X + lax.rem(x + dx, X), ch)

    hops = [(d, 0, 0) for d in (1, 2, 3)], [(0, d, 0) for d in (1, 2, 3)]
    twin = at(0, 0, 1)
    pair = lon - x
    mate = (lon, xh * 2 + 1 - core)
    far = (pair + 1 - x, (1 - xh) * 2 + core)
    outer = [(lax.rem(pair + step, lons), ch) for step in (lons - 2, lons - 1, 2, 3)]
    halo_to = [(lax.rem(pair + lons - 2 + 4 * x + i, lons), ch) for i in range(2)]

    def load_w(chip, who):
        columns = aligned((chip * 2 + who) * in_rows, 128, in_rows)
        return pltpu.make_async_copy(w_hbm.at[:, columns], wcol.at[pl.ds(0, 3 * taps)], load_sem.at[0])

    load_f = pltpu.make_async_copy(feat_hbm, raw.at[core], load_sem.at[1])
    loads = [
        pltpu.make_async_copy(cot_hbm.at[k], ext.at[pl.ds(BASES[k] + d + x * cols, cols)], load_sem.at[2 + k])
        for k, d in enumerate(DILATIONS)
    ]
    for copy in loads:
        copy.start()
    load_f.start()
    load_w(1 - xh, 1 - core).start()

    barrier = pltpu.get_barrier_semaphore()
    peers = [at(*hop) for hop in hops[0] + hops[1]] + [twin, mate, far] + outer
    for peer in peers:
        pl.semaphore_signal(barrier, inc=1, device_id=peer, device_id_type=MESH)
    pl.semaphore_wait(barrier, len(peers))

    def remote(src, dst, send, recv, peer):
        return pltpu.make_async_remote_copy(
            src_ref=src, dst_ref=dst, send_sem=send, recv_sem=recv, device_id=peer, device_id_type=MESH
        )

    inputs = []
    for k, d in enumerate(DILATIONS):
        base = BASES[k]
        start = (1 - x) * (cols - d)
        mine = remote(
            cot_hbm.at[k, pl.ds(start, d)],
            ext.at[pl.ds(base + d + x * cols + start, d)],
            halo_send.at[3 * k],
            halo_recv.at[3 * k],
            twin,
        )
        edges = [
            remote(
                cot_hbm.at[k, pl.ds(x * (cols - d), d)],
                ext.at[pl.ds(base + (1 - x) * (2 * cols + d), d)],
                halo_send.at[3 * k + 1 + i],
                halo_recv.at[3 * k + 1 + (1 - x)],
                halo_to[i],
            )
            for i in range(2)
        ]
        for copy in edges + [mine]:
            copy.start()
        before = ext.at[pl.ds(base, d)]
        after = ext.at[pl.ds(base + 2 * cols + d, d)]
        arrivals = [
            remote(before, before, halo_send.at[3 * k + 1], halo_recv.at[3 * k + 1], halo_to[0]),
            remote(after, after, halo_send.at[3 * k + 1], halo_recv.at[3 * k + 2], halo_to[0]),
        ]
        inputs.append((mine, edges, arrivals))
    rests = []
    for k, d in enumerate(DILATIONS[:2]):
        rests.append(
            remote(
                cot_hbm.at[k, pl.ds(x * d, cols - d)],
                ext.at[pl.ds(BASES[k] + d + x * cols + x * d, cols - d)],
                halo_send.at[9 + k],
                halo_recv.at[9 + k],
                twin,
            )
        )
        rests[k].start()
    feat_mate = remote(feat_hbm, raw.at[core], feat_send.at[0], feat_recv.at[0], mate)
    feat_far = remote(feat_hbm, raw.at[2 + core], feat_send.at[1], feat_recv.at[1], far)
    feat_on = remote(raw.at[2 + core], raw.at[2 + core], feat_send.at[2], feat_recv.at[2], mate)
    feat_mate.start()
    feat_far.start()

    lane = lax.broadcasted_iota(jnp.int32, (out_rows, 128), 1)

    def build(k, side, slot):
        d, base = DILATIONS[k], BASES[k]

        def column(m, carry):
            for lon_tap in range(3):
                v = ext[base + d + side * cols + m - d * (lon_tap - 1)]
                for lat_tap in range(3):
                    if lat_tap == 0:
                        moved = pltpu.roll(v, 128 - d, 1) * (lane < 128 - d).astype(v.dtype)
                    elif lat_tap == 1:
                        moved = v
                    else:
                        moved = pltpu.roll(v, d, 1) * (lane >= d).astype(v.dtype)
                    row = slot * taps + (lat_tap * 3 + lon_tap) * out_rows
                    stack[pl.ds(row, out_rows), aligned(m * 128, 128, 128)] = moved
            return carry

        lax.fori_loop(0, cols, column, 0)

    def flatten(chip):
        def column(m, carry):
            for jj in range(2):
                flat[pl.ds(jj * in_rows, in_rows), aligned(m * 128, 128, 128)] = raw[chip * 2 + jj, m]
            return carry

        lax.fori_loop(0, cols, column, 0)

    def order(e):
        return e >= 3, lax.rem(e, 3)

    def tile(h, block, sub, e):
        return part.at[e, aligned(mod4(here[h] + block) * rows, 8, rows), pl.ds(h * 256 + sub * 128, 128)]

    def rs1(e, h):
        up, down = at(*hops[h][0]), at(*hops[h][2])

        def send(i, src, peer):
            return remote(src, first.at[e, h, i], sum_send.at[e, h * 6 + i], sum_recv.at[e, h * 6 + i], peer)

        through = [send(0, tile(h, 2, 0, e), up), send(1, tile(h, 2, 1, e), down)]
        alone = [send(2, tile(h, 1, 1, e), up), send(3, tile(h, 3, 0, e), down)]
        both = [send(4, tile(h, 1, 0, e), up), send(5, tile(h, 3, 1, e), down)]
        return through, alone, both

    def piece(h, q, base_row=0, base_col=0):
        return (
            aligned(base_row + here[h] * rows + (q // 2) * (rows // 2), 8, rows // 2),
            aligned(base_col + h * 256 + lax.rem(q, 2) * 128, 128, 128),
        )

    def rs2(e, h):
        out = []
        for d in range(3):
            q = mod4(here[1 - h] + d + 1)
            slot = 12 + h * 3 + d
            r, c = piece(h, q)
            out.append(
                remote(part.at[e, r, c], second.at[e, h, d], sum_send.at[e, slot], sum_recv.at[e, slot], at(*hops[1 - h][d]))
            )
        return out

    def swap(e, h):
        return remote(low.at[e, h], third.at[e, h], sum_send.at[e, 18 + h], sum_recv.at[e, 18 + h], at(0, 0, 1))

    def corner(e):
        far_side, k = order(e)
        return k * taps, jnp.where(far_side, 1 - xh, xh) * 512

    def ag2_local(e, h):
        r, c = piece(h, here[1 - h], *corner(e))
        return pltpu.make_async_copy(low.at[e, h], kg_hbm.at[r, c], load_sem.at[5 + 2 * e + h])

    def ag2(e, h):
        r, c = piece(h, here[1 - h], *corner(e))
        return [
            remote(
                low.at[e, h], kg_hbm.at[r, c], sum_send.at[e, 20 + h * 3 + d], sum_recv.at[e, 20 + h * 3 + d], at(*hops[1 - h][d])
            )
            for d in range(3)
        ]

    def ag1(e, h):
        base_row, base_col = corner(e)
        up, down = at(*hops[h][0]), at(*hops[h][2])

        def send(i, block, sub, width, peer):
            area = kg_hbm.at[
                aligned(base_row + mod4(here[h] + block) * rows, 8, rows),
                aligned(base_col + h * 256 + sub * 128, 128, width),
            ]
            return remote(area, area, sum_send.at[e, 26 + h * 4 + i], sum_recv.at[e, 26 + h * 4 + i], peer)

        near = [send(0, 0, 0, 256, up), send(1, 0, 0, 256, down)]
        onward = [send(2, 3, 0, 128, up), send(3, 1, 1, 128, down)]
        return near, onward

    def do_chunk(e):
        far_side, k = order(e)
        slot = jnp.where(far_side, k, 3)
        for h in range(2):
            part[e, :, pl.ds(h * 256, 256)] = lax.dot_general(
                stack[aligned(slot * taps, 16, taps), :],
                flat[pl.ds(h * 256, 256), :],
                (((1,), (1,)), ((), ())),
                preferred_element_type=jnp.float32,
            )
            through, alone, _ = rs1(e, h)
            for copy in through + alone:
                copy.start()

    def do_rs1(e):
        for h in range(2):
            through, _, both = rs1(e, h)
            for i in range(2):
                through[i].wait()
                block, cols_at = (1, 3)[i], pl.ds(h * 256 + i * 128, 128)

                def step(n, carry):
                    r = aligned(mod4(here[h] + block) * rows + n * 16, 8, 16)
                    part[e, r, cols_at] = part[e, r, cols_at] + first[e, h, i, aligned(n * 16, 16, 16), :]
                    return carry

                lax.fori_loop(0, rows // 16, step, 0)
                both[i].start()

    def do_rs2(e):
        for h in range(2):
            _, alone, both = rs1(e, h)
            for copy in alone + both:
                copy.wait()

            def step(n, carry):
                r = aligned(n * 16, 16, 16)
                mine = aligned(here[h] * rows + n * 16, 8, 16)
                for sub, (a, b) in enumerate(((3, 4), (2, 5))):
                    c = pl.ds(h * 256 + sub * 128, 128)
                    part[e, mine, c] = part[e, mine, c] + (first[e, h, a, r, :] + first[e, h, b, r, :])
                return carry

            lax.fori_loop(0, rows // 16, step, 0)
            for copy in rs2(e, h):
                copy.start()

    def do_swap(e):
        for h in range(2):
            for copy in rs2(e, h):
                copy.wait()
            r, c = piece(h, here[1 - h])
            low[e, h] = (part[e, r, c] + second[e, h, 0]) + (second[e, h, 1] + second[e, h, 2])
            swap(e, h).start()

    def do_ag2(e):
        for h in range(2):
            swap(e, h).wait()
            low[e, h] = (low[e, h] + third[e, h]) * scale
            ag2_local(e, h).start()
            for copy in ag2(e, h):
                copy.start()

    def do_ag1(e):
        for h in range(2):
            ag2_local(e, h).wait()
            for copy in ag2(e, h):
                copy.wait()
            for copy in ag1(e, h)[0]:
                copy.start()

    def do_onward(e):
        for h in range(2):
            near, onward = ag1(e, h)
            near[1].wait_send()
            near[0].wait()
            onward[0].start()
            near[1].wait_recv()
            onward[1].start()

    def do_end(e):
        for h in range(2):
            for copy in ag1(e, h)[1]:
                copy.wait()

    wide = cols // GROUPS

    def turn(slot):
        wt[slot] = wcol[...].T

    def ig_group(slot, dst, q):
        def tile_of(i, carry):
            m = q * (wide // 2) + i
            res = jnp.dot(
                wt[slot], stack[pl.ds(0, wt.shape[2]), aligned(m * 256, 256, 256)], preferred_element_type=jnp.float32
            )
            prod[dst, 2 * m] = res[:, :128]
            prod[dst, 2 * m + 1] = res[:, 128:]
            return carry

        lax.fori_loop(0, wide // 2, tile_of, 0)

    def ig_mate(part_of, q):
        group = pl.ds(q * wide, wide)
        slot = part_of * GROUPS + q
        return remote(prod.at[0, group], other.at[part_of, group], ig_send.at[slot], ig_recv.at[slot], mate)

    def ig_far(q):
        group = pl.ds(q * wide, wide)
        slot = 2 * GROUPS + q
        return remote(prod.at[1, group], across.at[group], ig_send.at[slot], ig_recv.at[slot], far)

    def finish_far(q):
        ig_mate(1, q).wait()

        def column(i, carry):
            m = q * wide + i
            prod[1, m] = prod[1, m] + other[1, m]
            return carry

        lax.fori_loop(0, wide, column, 0)
        ig_far(q).start()

    def far_group(q):
        ig_group(0, 0, q)
        ig_mate(1, q).start()
        ig_group(1, 1, q)

        @pl.when(q > 0)
        def _():
            finish_far(q - 1)

    pad = wcol.shape[0] - 3 * taps
    wcol[pl.ds(3 * taps, pad), :] = jnp.zeros((pad, wcol.shape[1]), wcol.dtype)
    load_w(1 - xh, 1 - core).wait()
    turn(0)
    load_w(1 - xh, core).start()
    load_w(1 - xh, core).wait()
    turn(1)
    load_w(xh, 1 - core).start()

    def arrived(k):
        mine, edges, arrivals = inputs[k]
        loads[k].wait()
        mine.wait_recv()
        for copy in arrivals:
            copy.wait_recv()

    def body(s, carry):
        @pl.when(s == 0)
        def _():
            load_f.wait()
            feat_mate.wait()
            flatten(0)
            arrived(0)
            build(0, x, 3)

        @pl.when((s >= 1) & (s <= 3))
        def _():
            do_rs1(s - 1)

        @pl.when(s == 1)
        def _():
            arrived(1)
            build(1, x, 3)

        @pl.when(s == 2)
        def _():
            arrived(2)
            build(2, x, 3)

        @pl.when(s == 3)
        def _():
            feat_far.wait()
            feat_on.start()
            for k in range(3):
                if k < 2:
                    rests[k].wait()
                build(k, 1 - x, k)
            feat_on.wait()
            flatten(1)

        @pl.when(s < CHUNKS)
        def _():
            do_chunk(s)

        @pl.when((s >= 3) & (s < 3 + GROUPS))
        def _():
            far_group(s - 3)

        @pl.when(s == 3 + GROUPS)
        def _():
            finish_far(GROUPS - 1)

        @pl.when(s == 7)
        def _():
            load_w(xh, 1 - core).wait()
            turn(0)
            load_w(xh, core).start()
            for k in range(3):
                build(k, x, k)
            load_w(xh, core).wait()
            turn(1)

        @pl.when((s >= 8) & (s < 8 + GROUPS))
        def _():
            q = s - 8
            ig_group(0, 0, q)
            ig_mate(0, q).start()
            ig_group(1, 2, q)

        for lag, work in zip(LAG, (do_rs1, do_rs2, do_swap, do_ag2, do_ag1, do_onward)):
            u = s - lag
            late = (u >= 3) & (u < CHUNKS)
            ahead = (u >= -1) & (u < 2)

            @pl.when(late if lag == 1 else late | ahead)
            def _():
                work(jnp.where(u < 2, u + 1, u))

        return carry

    lax.fori_loop(0, CHUNKS + LAG[-1], body, 0)

    def last(q, carry):
        ig_mate(0, q).wait()
        ig_far(q).wait()

        def column(i, inner):
            m = q * wide + i
            ig[m] = (prod[2, m] + other[0, m] + across[m]).astype(jnp.bfloat16)
            return inner

        lax.fori_loop(0, wide, column, 0)
        return carry

    lax.fori_loop(0, GROUPS, last, 0)
    store = pltpu.make_async_copy(ig, ig_hbm, load_sem.at[0])
    store.start()
    for mine, edges, _ in inputs:
        mine.wait_send()
        for copy in edges:
            copy.wait_send()

    def end(e, carry):
        do_end(e)
        return carry

    lax.fori_loop(0, CHUNKS, end, 0)
    store.wait()


def local(features, cotangent, weights):
    in_rows, _, cols, lats = features.shape
    out_rows, in_total = weights.shape[3:]
    cells = cols * lats
    taps = 9 * out_rows
    rows = taps // 4
    depth = -(-3 * taps // 256) * 256
    scale = 1.0 / math.sqrt(cells * lax.axis_size("lon"))
    f32, bf16 = jnp.float32, jnp.bfloat16
    anywhere = pl.BlockSpec(memory_space=pl.ANY)
    ig, kg = pl.pallas_call(
        functools.partial(backward_kernel, scale),
        out_shape=(
            pltpu.VMEM((cols, in_rows, lats), bf16),
            pltpu.VMEM((3 * taps, in_total), f32),
        ),
        in_specs=[anywhere] * 3,
        out_specs=(anywhere, anywhere),
        scratch_shapes=[
            pltpu.VMEM((180, out_rows, lats), bf16),
            pltpu.VMEM((4 * taps, cells), bf16),
            pltpu.VMEM((4, cols, in_rows, lats), bf16),
            pltpu.VMEM((2 * in_rows, cells), bf16),
            pltpu.VMEM((depth, in_rows), bf16),
            pltpu.VMEM((2, in_rows, depth), bf16),
            pltpu.VMEM((CHUNKS, taps, 512), f32),
            pltpu.VMEM((CHUNKS, 2, 6, rows, 128), f32),
            pltpu.VMEM((CHUNKS, 2, 3, rows // 2, 128), f32),
            pltpu.VMEM((CHUNKS, 2, rows // 2, 128), f32),
            pltpu.VMEM((CHUNKS, 2, rows // 2, 128), f32),
            pltpu.VMEM((3, cols, in_rows, lats), f32),
            pltpu.VMEM((2, cols, in_rows, lats), f32),
            pltpu.VMEM((cols, in_rows, lats), f32),
            pltpu.VMEM((cols, in_rows, lats), bf16),
            pltpu.SemaphoreType.DMA((5 + 2 * CHUNKS,)),
            pltpu.SemaphoreType.DMA((11,)),
            pltpu.SemaphoreType.DMA((11,)),
            pltpu.SemaphoreType.DMA((3,)),
            pltpu.SemaphoreType.DMA((3,)),
            pltpu.SemaphoreType.DMA((CHUNKS, 34)),
            pltpu.SemaphoreType.DMA((CHUNKS, 34)),
            pltpu.SemaphoreType.DMA((3 * GROUPS,)),
            pltpu.SemaphoreType.DMA((3 * GROUPS,)),
        ],
        compiler_params=pltpu.CompilerParams(
            collective_id=1, has_side_effects=True, vmem_limit_bytes=52 * 1024 * 1024
        ),
        name="backward",
    )(
        features.reshape(in_rows, cols, lats).transpose(1, 0, 2),
        cotangent.reshape(3, out_rows, cols, lats).transpose(0, 2, 1, 3),
        weights.reshape(3 * taps, in_total),
    )
    input_grad = ig.transpose(1, 0, 2).reshape(in_rows, 1, cols, lats)
    return (input_grad, kg.reshape(3, 3, 3, out_rows, in_total))


def solution(mesh):
    return jax.shard_map(
        local,
        mesh=mesh,
        in_specs=(
            P("ch", None, "lon", None),
            P(None, "ch", None, "lon", None),
            P(None, None, None, "ch", None),
        ),
        out_specs=(P("ch", None, "lon", None), P(None, None, None, "ch", None)),
        check_vma=False,
    )
```

```python
import functools
import math

import jax
import jax.numpy as jnp
from jax import lax
from jax.experimental import pallas as pl
from jax.experimental.pallas import tpu as pltpu
from jax.sharding import PartitionSpec as P

DILATIONS = (6, 12, 18)
BASES = (0, 48, 108)
MESH = pl.DeviceIdType.MESH
Y, Z, X = 4, 4, 2
CHUNKS = 6
LAG = (1, 2, 3, 4, 5, 6)
GROUPS = 3


def mod4(v):
    return lax.rem(v, 4)


def aligned(v, m, size):
    return pl.ds(pl.multiple_of(v, m), size)


def backward_kernel(
    scale, feat_hbm, cot_hbm, w_hbm, ig_hbm, kg_hbm,
    ext, stack, raw, flat, wcol, wt, part, first, second, low, third, prod, other, across, ig,
    load_sem, halo_send, halo_recv, feat_send, feat_recv, sum_send, sum_recv, ig_send, ig_recv,
):
    lon = lax.axis_index("lon")
    ch = lax.axis_index("ch")
    lons = Y * Z * X
    y, z, x = lon // (Z * X), lax.rem(lon // X, Z), lax.rem(lon, X)
    xh, core = ch // 2, lax.rem(ch, 2)
    cols = feat_hbm.shape[0]
    in_rows = feat_hbm.shape[1]
    out_rows = cot_hbm.shape[2]
    taps = 9 * out_rows
    rows = taps // 4
    here = (y, z)

    def at(dy, dz, dx):
        return (mod4(y + dy) * (Z * X) + mod4(z + dz) * X + lax.rem(x + dx, X), ch)

    hops = [(d, 0, 0) for d in (1, 2, 3)], [(0, d, 0) for d in (1, 2, 3)]
    twin = at(0, 0, 1)
    pair = lon - x
    mate = (lon, xh * 2 + 1 - core)
    far = (pair + 1 - x, (1 - xh) * 2 + core)
    outer = [(lax.rem(pair + step, lons), ch) for step in (lons - 2, lons - 1, 2, 3)]
    halo_to = [(lax.rem(pair + lons - 1 + 3 * x, lons), ch), (lax.rem(pair + lons - 2 + 5 * x, lons), ch)]

    def load_w(chip, who):
        columns = aligned((chip * 2 + who) * in_rows, 128, in_rows)
        return pltpu.make_async_copy(w_hbm.at[:, columns], wcol.at[pl.ds(0, 3 * taps)], load_sem.at[0])

    load_f = pltpu.make_async_copy(feat_hbm, raw.at[core], load_sem.at[1])
    loads = [
        pltpu.make_async_copy(cot_hbm.at[k], ext.at[pl.ds(BASES[k] + d + x * cols, cols)], load_sem.at[2 + k])
        for k, d in enumerate(DILATIONS)
    ]
    for copy in loads:
        copy.start()
    load_f.start()
    load_w(1 - xh, 1 - core).start()

    barrier = pltpu.get_barrier_semaphore()
    peers = [at(*hop) for hop in hops[0] + hops[1]] + [twin, mate, far] + outer
    for peer in peers:
        pl.semaphore_signal(barrier, inc=1, device_id=peer, device_id_type=MESH)
    pl.semaphore_wait(barrier, len(peers))

    def remote(src, dst, send, recv, peer):
        return pltpu.make_async_remote_copy(
            src_ref=src, dst_ref=dst, send_sem=send, recv_sem=recv, device_id=peer, device_id_type=MESH
        )

    inputs = []
    for k, d in enumerate(DILATIONS):
        base = BASES[k]
        start = (1 - x) * (cols - d)
        mine = remote(
            cot_hbm.at[k, pl.ds(start, d)],
            ext.at[pl.ds(base + d + x * cols + start, d)],
            halo_send.at[3 * k],
            halo_recv.at[3 * k],
            twin,
        )
        edges = [
            remote(
                cot_hbm.at[k, pl.ds(x * (cols - d), d)],
                ext.at[pl.ds(base + (1 - x) * (2 * cols + d), d)],
                halo_send.at[3 * k + 1 + i],
                halo_recv.at[3 * k + 1 + (1 - x)],
                halo_to[i],
            )
            for i in range(2)
        ]
        for copy in (edges[0], mine):
            copy.start()
        arrivals = []
        for i, side in enumerate((x, 1 - x)):
            rim = ext.at[pl.ds(base + side * (2 * cols + d), d)]
            arrivals.append(remote(rim, rim, halo_send.at[3 * k + 1 + i], halo_recv.at[3 * k + 1 + side], halo_to[i]))
        inputs.append((mine, edges, arrivals))
    rests = []
    for k, d in enumerate(DILATIONS[:2]):
        rests.append(
            remote(
                cot_hbm.at[k, pl.ds(x * d, cols - d)],
                ext.at[pl.ds(BASES[k] + d + x * cols + x * d, cols - d)],
                halo_send.at[9 + k],
                halo_recv.at[9 + k],
                twin,
            )
        )
        rests[k].start()
    for k in range(3):
        inputs[k][1][1].start()
    feat_mate = remote(feat_hbm, raw.at[core], feat_send.at[0], feat_recv.at[0], mate)
    feat_far = remote(feat_hbm, raw.at[2 + core], feat_send.at[1], feat_recv.at[1], far)
    feat_on = remote(raw.at[2 + core], raw.at[2 + core], feat_send.at[2], feat_recv.at[2], mate)
    feat_mate.start()
    feat_far.start()

    lane = lax.broadcasted_iota(jnp.int32, (out_rows, 128), 1)

    def build(k, side, slot):
        d, base = DILATIONS[k], BASES[k]

        def column(m, carry):
            for lon_tap in range(3):
                v = ext[base + d + side * cols + m - d * (lon_tap - 1)]
                for lat_tap in range(3):
                    if lat_tap == 0:
                        moved = pltpu.roll(v, 128 - d, 1) * (lane < 128 - d).astype(v.dtype)
                    elif lat_tap == 1:
                        moved = v
                    else:
                        moved = pltpu.roll(v, d, 1) * (lane >= d).astype(v.dtype)
                    row = slot * taps + (lat_tap * 3 + lon_tap) * out_rows
                    stack[pl.ds(row, out_rows), aligned(m * 128, 128, 128)] = moved
            return carry

        lax.fori_loop(0, cols, column, 0)

    def flatten(chip):
        def column(m, carry):
            for jj in range(2):
                flat[pl.ds(jj * in_rows, in_rows), aligned(m * 128, 128, 128)] = raw[chip * 2 + jj, m]
            return carry

        lax.fori_loop(0, cols, column, 0)

    def order(e):
        return e >= 3, lax.rem(e, 3)

    def tile(h, block, sub, e):
        return part.at[e, aligned(mod4(here[h] + block) * rows, 8, rows), pl.ds(h * 256 + sub * 128, 128)]

    def rs1(e, h):
        up, down = at(*hops[h][0]), at(*hops[h][2])

        def send(i, src, peer):
            return remote(src, first.at[e, h, i], sum_send.at[e, h * 6 + i], sum_recv.at[e, h * 6 + i], peer)

        through = [send(0, tile(h, 2, 0, e), up), send(1, tile(h, 2, 1, e), down)]
        alone = [send(2, tile(h, 1, 1, e), up), send(3, tile(h, 3, 0, e), down)]
        both = [send(4, tile(h, 1, 0, e), up), send(5, tile(h, 3, 1, e), down)]
        return through, alone, both

    def piece(h, q, base_row=0, base_col=0):
        return (
            aligned(base_row + here[h] * rows + (q // 2) * (rows // 2), 8, rows // 2),
            aligned(base_col + h * 256 + lax.rem(q, 2) * 128, 128, 128),
        )

    def rs2(e, h):
        out = []
        for d in range(3):
            q = mod4(here[1 - h] + d + 1)
            slot = 12 + h * 3 + d
            r, c = piece(h, q)
            out.append(
                remote(part.at[e, r, c], second.at[e, h, d], sum_send.at[e, slot], sum_recv.at[e, slot], at(*hops[1 - h][d]))
            )
        return out

    def swap(e, h):
        return remote(low.at[e, h], third.at[e, h], sum_send.at[e, 18 + h], sum_recv.at[e, 18 + h], at(0, 0, 1))

    def corner(e):
        far_side, k = order(e)
        return k * taps, jnp.where(far_side, 1 - xh, xh) * 512

    def ag2_local(e, h):
        r, c = piece(h, here[1 - h], *corner(e))
        return pltpu.make_async_copy(low.at[e, h], kg_hbm.at[r, c], load_sem.at[5 + 2 * e + h])

    def ag2(e, h):
        r, c = piece(h, here[1 - h], *corner(e))
        return [
            remote(
                low.at[e, h], kg_hbm.at[r, c], sum_send.at[e, 20 + h * 3 + d], sum_recv.at[e, 20 + h * 3 + d], at(*hops[1 - h][d])
            )
            for d in range(3)
        ]

    def ag1(e, h):
        base_row, base_col = corner(e)
        up, down = at(*hops[h][0]), at(*hops[h][2])

        def send(i, block, sub, width, peer):
            area = kg_hbm.at[
                aligned(base_row + mod4(here[h] + block) * rows, 8, rows),
                aligned(base_col + h * 256 + sub * 128, 128, width),
            ]
            return remote(area, area, sum_send.at[e, 26 + h * 4 + i], sum_recv.at[e, 26 + h * 4 + i], peer)

        near = [send(0, 0, 0, 256, up), send(1, 0, 0, 256, down)]
        onward = [send(2, 3, 0, 128, up), send(3, 1, 1, 128, down)]
        return near, onward

    def do_chunk(e):
        far_side, k = order(e)
        slot = jnp.where(far_side, k, 3)
        for h in range(2):
            part[e, :, pl.ds(h * 256, 256)] = lax.dot_general(
                stack[aligned(slot * taps, 16, taps), :],
                flat[pl.ds(h * 256, 256), :],
                (((1,), (1,)), ((), ())),
                preferred_element_type=jnp.float32,
            )
            through, alone, _ = rs1(e, h)
            for copy in through + alone:
                copy.start()

    def do_rs1(e):
        for h in range(2):
            through, _, both = rs1(e, h)
            for i in range(2):
                through[i].wait()
                block, cols_at = (1, 3)[i], pl.ds(h * 256 + i * 128, 128)

                def step(n, carry):
                    r = aligned(mod4(here[h] + block) * rows + n * 16, 8, 16)
                    part[e, r, cols_at] = part[e, r, cols_at] + first[e, h, i, aligned(n * 16, 16, 16), :]
                    return carry

                lax.fori_loop(0, rows // 16, step, 0)
                both[i].start()

    def do_rs2(e):
        for h in range(2):
            _, alone, both = rs1(e, h)
            for copy in alone + both:
                copy.wait()

            def step(n, carry):
                r = aligned(n * 16, 16, 16)
                mine = aligned(here[h] * rows + n * 16, 8, 16)
                for sub, (a, b) in enumerate(((3, 4), (2, 5))):
                    c = pl.ds(h * 256 + sub * 128, 128)
                    part[e, mine, c] = part[e, mine, c] + (first[e, h, a, r, :] + first[e, h, b, r, :])
                return carry

            lax.fori_loop(0, rows // 16, step, 0)
            for copy in rs2(e, h):
                copy.start()

    def do_swap(e):
        for h in range(2):
            for copy in rs2(e, h):
                copy.wait()
            r, c = piece(h, here[1 - h])
            low[e, h] = (part[e, r, c] + second[e, h, 0]) + (second[e, h, 1] + second[e, h, 2])
            swap(e, h).start()

    def do_ag2(e):
        for h in range(2):
            swap(e, h).wait()
            low[e, h] = (low[e, h] + third[e, h]) * scale
            ag2_local(e, h).start()
            for copy in ag2(e, h):
                copy.start()

    def do_ag1(e):
        for h in range(2):
            ag2_local(e, h).wait()
            for copy in ag2(e, h):
                copy.wait()
            for copy in ag1(e, h)[0]:
                copy.start()

    def do_onward(e):
        for h in range(2):
            near, onward = ag1(e, h)
            near[1].wait_send()
            near[0].wait()
            onward[0].start()
            near[1].wait_recv()
            onward[1].start()

    def do_end(e):
        for h in range(2):
            for copy in ag1(e, h)[1]:
                copy.wait()

    wide = cols // GROUPS

    def turn(slot):
        wt[slot] = wcol[...].T

    def ig_group(slot, dst, q):
        def tile_of(i, carry):
            m = q * (wide // 2) + i
            res = jnp.dot(
                wt[slot], stack[pl.ds(0, wt.shape[2]), aligned(m * 256, 256, 256)], preferred_element_type=jnp.float32
            )
            prod[dst, 2 * m] = res[:, :128]
            prod[dst, 2 * m + 1] = res[:, 128:]
            return carry

        lax.fori_loop(0, wide // 2, tile_of, 0)

    def ig_mate(part_of, q):
        group = pl.ds(q * wide, wide)
        slot = part_of * GROUPS + q
        return remote(prod.at[0, group], other.at[part_of, group], ig_send.at[slot], ig_recv.at[slot], mate)

    def ig_far(q):
        group = pl.ds(q * wide, wide)
        slot = 2 * GROUPS + q
        return remote(prod.at[1, group], across.at[group], ig_send.at[slot], ig_recv.at[slot], far)

    def finish_far(q):
        ig_mate(1, q).wait()

        def column(i, carry):
            m = q * wide + i
            prod[1, m] = prod[1, m] + other[1, m]
            return carry

        lax.fori_loop(0, wide, column, 0)
        ig_far(q).start()

    def far_group(q):
        ig_group(0, 0, q)
        ig_mate(1, q).start()
        ig_group(1, 1, q)

        @pl.when(q > 0)
        def _():
            finish_far(q - 1)

    pad = wcol.shape[0] - 3 * taps
    wcol[pl.ds(3 * taps, pad), :] = jnp.zeros((pad, wcol.shape[1]), wcol.dtype)
    load_w(1 - xh, 1 - core).wait()
    turn(0)
    load_w(1 - xh, core).start()
    load_w(1 - xh, core).wait()
    turn(1)
    load_w(xh, 1 - core).start()

    def arrived(k):
        mine, edges, arrivals = inputs[k]
        loads[k].wait()
        mine.wait_recv()
        arrivals[0].wait_recv()

    def body(s, carry):
        @pl.when(s == 0)
        def _():
            load_f.wait()
            feat_mate.wait()
            flatten(0)
            arrived(0)
            build(0, x, 3)

        @pl.when(s == 1)
        def _():
            do_rs1(0)
            arrived(1)
            build(1, x, 3)

        @pl.when(s == 2)
        def _():
            arrived(2)
            build(2, x, 3)

        @pl.when(s == 3)
        def _():
            feat_far.wait()
            feat_on.start()
            for k in range(3):
                if k < 2:
                    rests[k].wait()
                inputs[k][2][1].wait_recv()
                build(k, 1 - x, k)
            feat_on.wait()
            flatten(1)

        @pl.when(s < CHUNKS)
        def _():
            do_chunk(s)

        @pl.when((s >= 3) & (s < 3 + GROUPS))
        def _():
            far_group(s - 3)

        @pl.when(s == 3 + GROUPS)
        def _():
            finish_far(GROUPS - 1)

        @pl.when(s == 7)
        def _():
            load_w(xh, 1 - core).wait()
            turn(0)
            load_w(xh, core).start()
            for k in range(3):
                build(k, x, k)
            load_w(xh, core).wait()
            turn(1)

        @pl.when((s >= 8) & (s < 8 + GROUPS))
        def _():
            q = s - 8
            ig_group(0, 0, q)
            ig_mate(0, q).start()
            ig_group(1, 2, q)

        for lag, work in zip(LAG, (do_rs1, do_rs2, do_swap, do_ag2, do_ag1, do_onward)):
            ahead = (s == lag - 1) if lag > 1 else False

            @pl.when(ahead | ((s > lag) & (s < CHUNKS + lag)))
            def _():
                work(jnp.where(s < lag, 0, s - lag))

        return carry

    lax.fori_loop(0, CHUNKS + LAG[-1], body, 0)

    def last(q, carry):
        ig_mate(0, q).wait()
        ig_far(q).wait()

        def column(i, inner):
            m = q * wide + i
            ig[m] = (prod[2, m] + other[0, m] + across[m]).astype(jnp.bfloat16)
            return inner

        lax.fori_loop(0, wide, column, 0)
        return carry

    lax.fori_loop(0, GROUPS, last, 0)
    store = pltpu.make_async_copy(ig, ig_hbm, load_sem.at[0])
    store.start()
    for mine, edges, _ in inputs:
        mine.wait_send()
        for copy in edges:
            copy.wait_send()

    def end(e, carry):
        do_end(e)
        return carry

    lax.fori_loop(0, CHUNKS, end, 0)
    store.wait()


def local(features, cotangent, weights):
    in_rows, _, cols, lats = features.shape
    out_rows, in_total = weights.shape[3:]
    cells = cols * lats
    taps = 9 * out_rows
    rows = taps // 4
    depth = -(-3 * taps // 256) * 256
    scale = 1.0 / math.sqrt(cells * lax.axis_size("lon"))
    f32, bf16 = jnp.float32, jnp.bfloat16
    anywhere = pl.BlockSpec(memory_space=pl.ANY)
    ig, kg = pl.pallas_call(
        functools.partial(backward_kernel, scale),
        out_shape=(
            pltpu.VMEM((cols, in_rows, lats), bf16),
            pltpu.VMEM((3 * taps, in_total), f32),
        ),
        in_specs=[anywhere] * 3,
        out_specs=(anywhere, anywhere),
        scratch_shapes=[
            pltpu.VMEM((180, out_rows, lats), bf16),
            pltpu.VMEM((4 * taps, cells), bf16),
            pltpu.VMEM((4, cols, in_rows, lats), bf16),
            pltpu.VMEM((2 * in_rows, cells), bf16),
            pltpu.VMEM((depth, in_rows), bf16),
            pltpu.VMEM((2, in_rows, depth), bf16),
            pltpu.VMEM((CHUNKS, taps, 512), f32),
            pltpu.VMEM((CHUNKS, 2, 6, rows, 128), f32),
            pltpu.VMEM((CHUNKS, 2, 3, rows // 2, 128), f32),
            pltpu.VMEM((CHUNKS, 2, rows // 2, 128), f32),
            pltpu.VMEM((CHUNKS, 2, rows // 2, 128), f32),
            pltpu.VMEM((3, cols, in_rows, lats), f32),
            pltpu.VMEM((2, cols, in_rows, lats), f32),
            pltpu.VMEM((cols, in_rows, lats), f32),
            pltpu.VMEM((cols, in_rows, lats), bf16),
            pltpu.SemaphoreType.DMA((5 + 2 * CHUNKS,)),
            pltpu.SemaphoreType.DMA((11,)),
            pltpu.SemaphoreType.DMA((11,)),
            pltpu.SemaphoreType.DMA((3,)),
            pltpu.SemaphoreType.DMA((3,)),
            pltpu.SemaphoreType.DMA((CHUNKS, 34)),
            pltpu.SemaphoreType.DMA((CHUNKS, 34)),
            pltpu.SemaphoreType.DMA((3 * GROUPS,)),
            pltpu.SemaphoreType.DMA((3 * GROUPS,)),
        ],
        compiler_params=pltpu.CompilerParams(
            collective_id=1, has_side_effects=True, vmem_limit_bytes=52 * 1024 * 1024
        ),
        name="backward",
    )(
        features.reshape(in_rows, cols, lats).transpose(1, 0, 2),
        cotangent.reshape(3, out_rows, cols, lats).transpose(0, 2, 1, 3),
        weights.reshape(3 * taps, in_total),
    )
    input_grad = ig.transpose(1, 0, 2).reshape(in_rows, 1, cols, lats)
    return (input_grad, kg.reshape(3, 3, 3, out_rows, in_total))


def solution(mesh):
    return jax.shard_map(
        local,
        mesh=mesh,
        in_specs=(
            P("ch", None, "lon", None),
            P(None, "ch", None, "lon", None),
            P(None, None, None, "ch", None),
        ),
        out_specs=(P("ch", None, "lon", None), P(None, None, None, "ch", None)),
        check_vma=False,
    )
```
